256 devices in a mesh: elec: 16 (over z_hi, x, core), space: 16 (over z_lo, y).
Axes of the slice: x: 4, y: 4, z: 8 (z_hi: 2, z_lo: 4; z = z_hi * 4 + z_lo), core: 2. Of those that a mesh axis runs over, the one named last changes fastest.
Arguments:
- potentials: bfloat16 [2048, 32, 8, 128], P('elec', 'space'), may hold values from -6 to 6
- quadrupoles: int32 [4, 32768], replicated, may hold values from 0 to 2047
- residuals: float32 [32768], replicated, may hold values from -0.03125 to 0.03125
- cell_weight: float32 [32, 8, 128], P('space'), may hold values from 0.5 to 2
Outputs:
- model_gradient: float32 [32, 8, 128], P('space')
The draws below stay inside these ranges and needn't reach their ends.
All inputs are finite; a program needn't handle non-finite values.
Results may differ from the reference program's by a relative error of at most 0.0054.
Values may be sent and summed in bfloat16 or wider, within the bound.
A program may use at most 192 MiB of HBM per device.

```python
import math
import jax
import jax.numpy as jnp
from jax import lax

E = 2048
NZ = 8
NY = 128
QUADS = 32768
NX = 32


def plant(entries, stream_key, smallest, top_value):
    place = [jax.random.randint(jax.random.fold_in(stream_key, axis), (), 0, length) for axis, length in enumerate(entries.shape)]
    main_axis = entries.shape.index(max(entries.shape))
    neighbour = place[:main_axis] + [(place[main_axis] + 1) % entries.shape[main_axis]] + place[main_axis + 1:]
    return entries.at[tuple(place)].set(smallest).at[tuple(neighbour)].set(top_value)


def steps_of(stream_key, dims, split, low, high):
    gain, own = 1.0, jax.random.fold_in(stream_key, 6)
    for dim, shards_of in split:
        steps = jnp.exp(jax.random.uniform(jax.random.fold_in(own, dim), (shards_of,), jnp.float32, low / len(split), high / len(split)))
        gain = gain * jnp.repeat(steps, dims[dim] // shards_of).reshape([-1 if axis == dim else 1 for axis in range(len(dims))])
    return gain


def normal_values(stream_key, shape, scale, reach, split=(), kind=jnp.bfloat16):
    factor_of = steps_of(stream_key, shape, split, -0.22, 0.18) if split else 1.0
    array = jax.random.normal(stream_key, shape, jnp.float32) * scale * factor_of
    return jnp.minimum(jnp.maximum(array, -reach), reach).astype(kind)


def setup_inputs(seed: int = 0) -> dict:
    key_of = jax.random.split(jax.random.key(seed), 5)
    potentials = normal_values(key_of[0], (E, NX, NZ, NY), 1.0, 6.0, ((0, 16), (1, 16)))
    quadrupoles = plant(jax.random.randint(key_of[1], (4, QUADS), 0, E), jax.random.fold_in(key_of[1], 1), 0, E - 1).astype(jnp.int32)
    residuals = normal_values(key_of[2], (QUADS,), QUADS ** -0.5, 0.03125, (), jnp.float32)
    cell_weight = jnp.clip(jnp.exp(math.log(2.0) - 1.3862944 * jax.random.uniform(key_of[3], (NX, NZ, NY), jnp.float32) ** steps_of(key_of[3], (NX, NZ, NY), ((0, 16),), -0.2, 0.2)), 0.5, 2.0)
    return {"potentials": potentials, "quadrupoles": quadrupoles, "residuals": residuals, "cell_weight": cell_weight}


def slopes_of(padded):
    field = padded.astype(jnp.float32)
    grad_x = 0.5 * (field[:, 2:] - field[:, :-2])
    inner = field[:, 1:-1]
    pad_z = jnp.pad(inner, ((0, 0), (0, 0), (1, 1), (0, 0)))
    grad_z = 0.5 * (pad_z[:, :, 2:] - pad_z[:, :, :-2])
    pad_y = jnp.pad(inner, ((0, 0), (0, 0), (0, 0), (1, 1)))
    grad_y = 0.5 * (pad_y[:, :, :, 2:] - pad_y[:, :, :, :-2])
    return jnp.stack([grad_x, grad_z, grad_y], axis=0).astype(jnp.bfloat16)


def coupling_rows(quadrupoles, residuals, first, count, width):
    source_a = quadrupoles[0]
    source_b = quadrupoles[1]
    probe_m = quadrupoles[2]
    probe_n = quadrupoles[3]
    rows = jnp.concatenate([source_a, source_a, source_b, source_b]) - first
    cols = jnp.concatenate([probe_m, probe_n, probe_m, probe_n])
    values = jnp.concatenate([residuals, -residuals, -residuals, residuals]).astype(jnp.float32)
    valid = (rows >= 0) & (rows < count)
    flat = jnp.where(valid, rows * width + cols, count * width).astype(jnp.int32)
    summed = jax.ops.segment_sum(values, flat, num_segments=count * width)
    return summed.reshape(count, width).astype(jnp.bfloat16)


def reference(potentials, quadrupoles, residuals, cell_weight):
    coupling = coupling_rows(quadrupoles, residuals, 0, E, E).astype(jnp.float32)
    padded = jnp.pad(potentials, ((0, 0), (1, 1), (0, 0), (0, 0)))

    def one_plane(index):
        window = lax.dynamic_slice_in_dim(padded, index, 3, 1)
        slopes = slopes_of(window).astype(jnp.float32)
        image = jnp.einsum("ef,kfxzy->kexzy", coupling, slopes, precision=lax.Precision.HIGHEST)
        return jnp.sum(slopes * image, axis=(0, 1))[0]

    planes = lax.map(one_plane, jnp.arange(NX, dtype=jnp.int32))
    return planes * cell_weight
```

```python
import jax
import jax.numpy as jnp
from jax import lax
from jax.experimental import pallas as pl
from jax.experimental.pallas import tpu as pltpu
from jax.sharding import PartitionSpec as P

MESH = pl.DeviceIdType.MESH
F32 = jnp.float32
BF16 = jnp.bfloat16
E = 2048
EL = 128
QUADS = 32768
QK = 2048
ROWS = 80
WIN = 1280
NC = 768


def kernel(pot, quad, res, weight, out,
           uf, lo, hi, hf, sb, S, Tb, gs, gr,
           halo_s, halo_r, fs, fr, ws, wr, z_s, z_r, p2_s, p2_r, p3_s, p3_r, g_s, g_r):
    e = lax.axis_index("elec")
    s = lax.axis_index("space")
    zh, x, c = e // 8, (e // 2) % 4, e % 2
    zl, y = s // 4, s % 4
    z = zh * 4 + zl
    mi = zh * 4 + x

    def elec_peer(k):
        return (lax.rem(e + k, 16), s)

    def space_peer(d):
        return (e, lax.rem(s + d + 16, 16))

    def z_peer(d):
        t = lax.rem(z + d, 8)
        return ((t // 4) * 8 + x * 2 + c, lax.rem(t, 4) * 4 + y)

    def x_peer(d):
        return (zh * 8 + lax.rem(x + d, 4) * 2 + c, s)

    def y_peer(d):
        return (e, zl * 4 + lax.rem(y + d, 4))

    other_core = (zh * 8 + x * 2 + (1 - c), s)

    def remote(src, dst, ss, rs, device):
        return pltpu.make_async_remote_copy(
            src_ref=src, dst_ref=dst, send_sem=ss, recv_sem=rs, device_id=device, device_id_type=MESH)

    barrier = pltpu.get_barrier_semaphore()
    peers = ([elec_peer(k) for k in range(1, 16)] + [space_peer(1), space_peer(-1)]
             + [z_peer(d) for d in (1, 2, 3, 5, 6, 7)] + [y_peer(d) for d in (1, 2, 3)])
    for peer in peers:
        pl.semaphore_signal(barrier, inc=1, device_id=peer, device_id_type=MESH)

    uf[...] = pot[...].astype(F32).reshape(EL * 16, 128)
    pl.semaphore_wait(barrier, len(peers))

    up = remote(pot.at[:, 1], lo, halo_s.at[0], halo_r.at[0], space_peer(1))
    down = remote(pot.at[:, 0], hi, halo_s.at[1], halo_r.at[1], space_peer(-1))
    up.start()
    down.start()

    lane = lax.broadcasted_iota(jnp.int32, (EL, 128), 1)

    def target(j):
        dz = jnp.where(j < 4, 1, 0)
        dx = jnp.where(j < 4, j, j - 3)
        return lax.rem(zh + dz, 2), lax.rem(x + dx, 4)

    def source(j):
        dz = jnp.where(j < 4, 1, 0)
        dx = jnp.where(j < 4, j, j - 3)
        return (lax.rem(zh + dz, 2) * 8 + lax.rem(x + 4 - lax.rem(dx, 4), 4) * 2 + c) * EL

    def field_copy(j, part):
        tz, tx = target(j)
        m = tz * 4 + tx
        cols = pl.ds(0, 512) if part == 0 else pl.ds(512, 256)
        return remote(sb.at[m, :, cols], S.at[pl.ds(pl.multiple_of(e * EL, EL), EL), cols],
                      fs.at[part, j], fr.at[part, j], (tz * 8 + tx * 2 + c, s))

    def column(ref, start, stride):
        return ref[pl.ds(start, EL, stride=stride), :]

    def zy_step(j, carry):
        tz, tx = target(j)
        m = tz * 4 + tx
        for p in range(2):
            u = column(uf, p * 8 + m, 16)
            before = jnp.where(m > 0, column(uf, p * 8 + jnp.maximum(m - 1, 0), 16), 0.0)
            after = jnp.where(m < 7, column(uf, p * 8 + jnp.minimum(m + 1, 7), 16), 0.0)
            left = jnp.where(lane > 0, pltpu.roll(u, 1, axis=1), 0.0)
            right = jnp.where(lane < 127, pltpu.roll(u, 127, axis=1), 0.0)
            sb[m, :, p * 128:p * 128 + 128] = (0.5 * (right - left)).astype(BF16)
            sb[m, :, 256 + p * 128:256 + p * 128 + 128] = (0.5 * (after - before)).astype(BF16)

        @pl.when(j < 7)
        def _():
            field_copy(j, 0).start()

        return carry

    lax.fori_loop(0, 8, zy_step, 0)

    rb = jnp.where(z < 4, y * 4 + x, x * 4 + y)
    col0 = c * 1024 + z * 128
    row0 = (c * 4 + z // 2) * 256 + rb * ROWS
    row_ids = ((lax.broadcasted_iota(jnp.int32, (ROWS, QK), 0) + row0) & (E - 1)).astype(jnp.int16)
    col_ids = (lax.broadcasted_iota(jnp.int32, (EL, QK), 0) + col0).astype(jnp.int16)
    one = jnp.ones((16, QK), BF16)
    zero = jnp.zeros((16, QK), BF16)

    def hot(u, v, ids, plus, minus):
        return jnp.concatenate(
            [jnp.where(u == ids[k:k + 16], plus, jnp.where(v == ids[k:k + 16], minus, zero))
             for k in range(0, ids.shape[0], 16)], axis=0)

    def nt(a, b):
        return lax.dot_general(a, b, (((1,), (1,)), ((), ())), preferred_element_type=F32)

    def quad_step(i, acc):
        q = pl.ds(pl.multiple_of(i * QK, QK), QK)
        a, b, m, n = (quad[k:k + 1, q] for k in range(4))
        r = jnp.where((a == b) | (m == n), 0.0, res[0:1, q])
        a, b, m, n = (jnp.broadcast_to(v, (16, QK)).astype(jnp.int16) for v in (a, b, m, n))
        r = jnp.broadcast_to(r, (16, QK)).astype(BF16)
        acc = acc + nt(hot(a, b, row_ids, one, -one), hot(m, n, col_ids, r, -r))
        return acc + nt(hot(m, n, row_ids, one, -one), hot(a, b, col_ids, r, -r))

    block = lax.fori_loop(0, QUADS // QK, quad_step, jnp.zeros((ROWS, EL), F32))
    offset = lax.broadcasted_iota(jnp.int32, (ROWS, EL), 0) + rb * ROWS
    block = jnp.where((offset < 256) | (offset >= 1024), 0.5 * block, block)
    own = pl.ds(pl.multiple_of(rb * ROWS, 16), ROWS)
    Tb[z, own, :] = block.astype(BF16)

    def z_copy(d):
        return remote(Tb.at[z, own], Tb.at[z, own], z_s.at[d - 1], z_r.at[d - 1], z_peer(d))

    for d in range(1, 8):
        z_copy(d).start()

    up.wait_recv()
    down.wait_recv()
    hf[0:EL * 8, :] = jnp.where(s > 0, lo[...].astype(F32).reshape(EL * 8, 128), 0.0)
    hf[EL * 8:, :] = jnp.where(s < 15, hi[...].astype(F32).reshape(EL * 8, 128), 0.0)

    def x_step(j, carry):
        tz, tx = target(j)
        m = tz * 4 + tx
        u0, u1 = column(uf, m, 16), column(uf, 8 + m, 16)
        low, high = column(hf, m, 8), column(hf, EL * 8 + m, 8)
        sb[m, :, 512:640] = (0.5 * (u1 - low)).astype(BF16)
        sb[m, :, 640:768] = (0.5 * (high - u0)).astype(BF16)

        @pl.when(j < 7)
        def _():
            field_copy(j, 1).start()

        return carry

    lax.fori_loop(0, 8, x_step, 0)

    def forward(j):
        rows = pl.ds(pl.multiple_of(source(j), EL), EL)
        return remote(S.at[rows], S.at[rows], ws.at[j], wr.at[j], other_core)

    S[pl.ds(pl.multiple_of(e * EL, EL), EL), :] = sb[mi]
    forward(7).start()

    slab_a = pl.ds(pl.multiple_of((y * 4 + x) * ROWS, 16), ROWS)
    slab_b = pl.ds(pl.multiple_of((x * 4 + y) * ROWS, 16), ROWS)
    wide_a = pl.ds(pl.multiple_of(y * 4 * ROWS, 16), 4 * ROWS)
    wide_b = pl.ds(pl.multiple_of(x * 4 * ROWS, 16), 4 * ROWS)

    def slab_copies(d):
        a, b = Tb.at[0:4, slab_a], Tb.at[4:8, slab_b]
        return (remote(a, a, p2_s.at[0, d - 1], p2_r.at[0, d - 1], x_peer(d)),
                remote(b, b, p2_s.at[1, d - 1], p2_r.at[1, d - 1], y_peer(d)))

    def wide_copies(d):
        a, b = Tb.at[0:4, wide_a], Tb.at[4:8, wide_b]
        return (remote(a, a, p3_s.at[0, d - 1], p3_r.at[0, d - 1], y_peer(d)),
                remote(b, b, p3_s.at[1, d - 1], p3_r.at[1, d - 1], x_peer(d)))

    for d in range(1, 8):
        z_copy(d).wait_recv()
    for d in range(1, 4):
        for copy in slab_copies(d):
            copy.start()

    def forward_step(j, carry):
        field_copy(j, 0).wait_recv()
        field_copy(j, 1).wait_recv()
        forward(j).start()
        return carry

    lax.fori_loop(4, 7, forward_step, 0)
    for d in range(1, 4):
        for copy in slab_copies(d):
            copy.wait_recv()
    for d in range(1, 4):
        for copy in wide_copies(d):
            copy.start()
    lax.fori_loop(0, 4, forward_step, 0)
    for d in range(1, 4):
        for copy in wide_copies(d):
            copy.wait_recv()

    def forwarded(j, carry):
        forward(j).wait_recv()
        return carry

    lax.fori_loop(0, 8, forwarded, 0)

    def block_step(jj, acc):
        lhs = jnp.concatenate([Tb[2 * jj], Tb[2 * jj + 1]], axis=1)
        first = c * 4 + jj
        sums = []
        for n in range(3):
            cols = slice(n * 256, n * 256 + 256)
            rhs = S[pl.ds(pl.multiple_of(first * 256, 256), 256), cols]
            image = jnp.dot(lhs, rhs, preferred_element_type=F32)
            total = jnp.zeros((8, 256), F32)
            for d in range(5):
                rows = pl.ds(pl.multiple_of(lax.rem(first + d, 8) * 256, 256), 256)
                prod = image[d * 256:d * 256 + 256] * S[rows, cols].astype(F32)
                total = total + jnp.sum(prod.reshape(32, 8, 256), axis=0)
            sums.append(total)
        return acc + (sums[0] + sums[1] + sums[2])

    total = lax.fori_loop(0, 4, block_step, jnp.zeros((8, 256), F32))
    total = jnp.sum(total, axis=0, keepdims=True)
    gs[...] = jnp.zeros((8, 128), F32)
    gs[0:1, :] = total[:, 0:128]
    gs[1:2, :] = total[:, 128:256]

    def share(k):
        return remote(gs, gr.at[e], g_s.at[k - 1], g_r.at[k - 1], elec_peer(k))

    for k in range(1, 16):
        share(k).start()
    gr[e] = gs[...]
    for k in range(1, 16):
        share(k).wait_recv()
    for m in range(8):
        both = gr[2 * m] + gr[2 * m + 1]
        for p in range(2):
            out[p, m:m + 1, :] = both[p:p + 1, :] * weight[p, m:m + 1, :]

    up.wait_send()
    down.wait_send()

    def sent(j, carry):
        field_copy(j, 0).wait_send()
        field_copy(j, 1).wait_send()
        return carry

    lax.fori_loop(0, 7, sent, 0)

    def passed(j, carry):
        forward(j).wait_send()
        return carry

    lax.fori_loop(0, 8, passed, 0)
    for d in range(1, 8):
        z_copy(d).wait_send()
    for d in range(1, 4):
        for copy in slab_copies(d) + wide_copies(d):
            copy.wait_send()
    for k in range(1, 16):
        share(k).wait_send()


def local(potentials, quadrupoles, residuals, cell_weight):
    dma = pltpu.SemaphoreType.DMA
    return pl.pallas_call(
        kernel,
        name="misfit_gradient",
        out_shape=jax.ShapeDtypeStruct(cell_weight.shape, F32),
        in_specs=[pl.BlockSpec(memory_space=pltpu.VMEM)] * 4,
        out_specs=pl.BlockSpec(memory_space=pltpu.VMEM),
        scratch_shapes=[
            pltpu.VMEM((EL * 16, 128), F32),
            pltpu.VMEM((EL, 8, 128), BF16),
            pltpu.VMEM((EL, 8, 128), BF16),
            pltpu.VMEM((EL * 16, 128), F32),
            pltpu.VMEM((8, EL, NC), BF16),
            pltpu.VMEM((E, NC), BF16),
            pltpu.VMEM((8, WIN, 128), BF16),
            pltpu.VMEM((8, 128), F32),
            pltpu.VMEM((16, 8, 128), F32),
            dma((2,)), dma((2,)),
            dma((2, 7)), dma((2, 7)),
            dma((8,)), dma((8,)),
            dma((7,)), dma((7,)),
            dma((2, 3)), dma((2, 3)),
            dma((2, 3)), dma((2, 3)),
            dma((15,)), dma((15,)),
        ],
        compiler_params=pltpu.CompilerParams(
            collective_id=0, has_side_effects=True, vmem_limit_bytes=56 << 20),
    )(potentials, quadrupoles, residuals.reshape(1, QUADS), cell_weight)


def solution(mesh):
    placed = (P("elec", "space", None, None), P(), P(), P("space", None, None))
    return jax.shard_map(
        local, mesh=mesh, in_specs=placed, out_specs=P("space", None, None), check_vma=False
    )
```

```python
import jax
import jax.numpy as jnp
from jax import lax
from jax.experimental import pallas as pl
from jax.experimental.pallas import tpu as pltpu
from jax.sharding import PartitionSpec as P

MESH = pl.DeviceIdType.MESH
F32 = jnp.float32
BF16 = jnp.bfloat16
E = 2048
EL = 128
QUADS = 32768
QK = 2048
ROWS = 80
WIN = 1280
NA = 6
PIECES = ((0, 0, 128), (1, 0, 64), (1, 64, 64))
NC = 768


def kernel(pot, quad, res, weight, out,
           uf, W, sr, H, sb, S, Tb, gs, gr,
           r_s, r_r, halo_s, halo_r, fs, fr, ws, wr, z_s, z_r, p2_s, p2_r, p3_s, p3_r, p4_s, p4_r, g_s, g_r):
    e = lax.axis_index("elec")
    s = lax.axis_index("space")
    zh, x, c = e // 8, (e // 2) % 4, e % 2
    zl, y = s // 4, s % 4
    z = zh * 4 + zl

    def elec_peer(k):
        return (lax.rem(e + k, 16), s)

    def space_peer(d):
        return (e, lax.rem(s + d + 16, 16))

    def z_peer(d):
        t = lax.rem(z + d, 8)
        return ((t // 4) * 8 + x * 2 + c, lax.rem(t, 4) * 4 + y)

    def x_peer(d):
        return (zh * 8 + lax.rem(x + d, 4) * 2 + c, s)

    def y_peer(d):
        return (e, zl * 4 + lax.rem(y + d, 4))

    other_core = (zh * 8 + x * 2 + (1 - c), s)
    partner = lax.rem(e + 8, 16)

    def remote(src, dst, ss, rs, device):
        return pltpu.make_async_remote_copy(
            src_ref=src, dst_ref=dst, send_sem=ss, recv_sem=rs, device_id=device, device_id_type=MESH)

    barrier = pltpu.get_barrier_semaphore()
    peers = ([elec_peer(k) for k in range(1, 16)] + [space_peer(1), space_peer(-1)]
             + [z_peer(d) for d in (1, 2, 3, 5, 6, 7)] + [y_peer(d) for d in (1, 2, 3)])
    for peer in peers:
        pl.semaphore_signal(barrier, inc=1, device_id=peer, device_id_type=MESH)

    uf[...] = pot[...].astype(F32).reshape(EL * 16, 128)

    def half_step(i, carry):
        for p in range(2):
            mine = zh * 4 + i - 1
            u = uf[pl.ds(p * 8 + jnp.clip(mine, 0, 7), EL, stride=16), :]
            W[0, i, p] = jnp.where((mine >= 0) & (mine < 8), u, 0.0).astype(BF16)
            theirs = (1 - zh) * 4 + i - 1
            sr[i, p] = uf[pl.ds(p * 8 + jnp.clip(theirs, 0, 7), EL, stride=16), :].astype(BF16)
        return carry

    lax.fori_loop(0, 6, half_step, 0)
    W[1, 5 * zh] = jnp.zeros((2, EL, 128), BF16)

    @pl.when(s == 0)
    def _():
        H[:, 0] = jnp.zeros((2, 4, EL, 128), BF16)

    @pl.when(s == 15)
    def _():
        H[:, 1] = jnp.zeros((2, 4, EL, 128), BF16)

    rb = jnp.where(z < NA, y * 4 + x, x * 4 + y)
    col0 = c * 1024 + z * 128
    row0 = (c * 4 + z // 2) * 256 + rb * ROWS
    row_ids = ((lax.broadcasted_iota(jnp.int32, (ROWS, QK), 0) + row0) & (E - 1)).astype(jnp.int16)
    col_ids = (lax.broadcasted_iota(jnp.int32, (EL, QK), 0) + col0).astype(jnp.int16)
    one = jnp.ones((16, QK), BF16)
    zero = jnp.zeros((16, QK), BF16)

    def hot(u, v, ids, plus, minus):
        return jnp.concatenate(
            [jnp.where(u == ids[k:k + 16], plus, jnp.where(v == ids[k:k + 16], minus, zero))
             for k in range(0, ids.shape[0], 16)], axis=0)

    def nt(a, b):
        return lax.dot_general(a, b, (((1,), (1,)), ((), ())), preferred_element_type=F32)

    def quad_step(i, acc):
        q = pl.ds(pl.multiple_of(i * QK, QK), QK)
        a, b, m, n = (quad[k:k + 1, q] for k in range(4))
        r = jnp.where((a == b) | (m == n), 0.0, res[0:1, q])
        a, b, m, n = (jnp.broadcast_to(v, (16, QK)).astype(jnp.int16) for v in (a, b, m, n))
        r = jnp.broadcast_to(r, (16, QK)).astype(BF16)
        acc = acc + nt(hot(a, b, row_ids, one, -one), hot(m, n, col_ids, r, -r))
        return acc + nt(hot(m, n, row_ids, one, -one), hot(a, b, col_ids, r, -r))

    block = lax.fori_loop(0, QUADS // QK, quad_step, jnp.zeros((ROWS, EL), F32))
    offset = lax.broadcasted_iota(jnp.int32, (ROWS, EL), 0) + rb * ROWS
    block = jnp.where((offset < 256) | (offset >= 1024), 0.5 * block, block)
    own = pl.ds(pl.multiple_of(rb * ROWS, 16), ROWS)
    Tb[z, own, :] = block.astype(BF16)

    pl.semaphore_wait(barrier, len(peers))

    raw = pl.ds(zh, 5)

    def raw_copy(i):
        _, lo, n = PIECES[i]
        return remote(sr.at[raw, :, lo:lo + n], W.at[1, raw, :, lo:lo + n], r_s.at[i - 1], r_r.at[i - 1], (partner, s))

    def halo_copies(i):
        g, lo, n = PIECES[i]
        return (remote(W.at[g, 1:5, 1, lo:lo + n], H.at[g, 0, :, lo:lo + n],
                       halo_s.at[i, 0], halo_r.at[i, 0], space_peer(1)),
                remote(W.at[g, 1:5, 0, lo:lo + n], H.at[g, 1, :, lo:lo + n],
                       halo_s.at[i, 1], halo_r.at[i, 1], space_peer(-1)))

    def start_halo(i):
        up, down = halo_copies(i)

        @pl.when(s < 15)
        def _():
            up.start()

        @pl.when(s > 0)
        def _():
            down.start()

    def halo_arrived(i):
        up, down = halo_copies(i)

        @pl.when(s > 0)
        def _():
            up.wait_recv()

        @pl.when(s < 15)
        def _():
            down.wait_recv()

    def halo_sent(i):
        up, down = halo_copies(i)

        @pl.when(s < 15)
        def _():
            up.wait_send()

        @pl.when(s > 0)
        def _():
            down.wait_send()

    def z_copy(d):
        return remote(Tb.at[z, own], Tb.at[z, own], z_s.at[d - 1], z_r.at[d - 1], z_peer(d))

    start_halo(0)
    for d in range(1, 8):
        z_copy(d).start()
    def electrodes(i, origin):
        _, lo, n = PIECES[i]
        return pl.ds(pl.multiple_of(origin * EL + lo, 64), n)

    def group(i):
        return e if PIECES[i][0] == 0 else partner

    def field_copy(i, d, part):
        g, lo, n = PIECES[i]
        tx = lax.rem(x + d, 4)
        cols = pl.ds(0, 512) if part == 0 else pl.ds(512, 256)
        return remote(sb.at[g, tx, lo:lo + n, cols], S.at[electrodes(i, group(i)), cols],
                      fs.at[i, part, d - 1], fr.at[i, part, d - 1], x_peer(d))

    def zy_slopes(i):
        g, lo, n = PIECES[i]
        rows = slice(lo, lo + n)
        lane = lax.broadcasted_iota(jnp.int32, (n, 128), 1)

        def step(j, carry):
            t = lax.rem(x + j, 4)
            for p in range(2):
                u = W[g, t + 1, p, rows].astype(F32)
                before, after = W[g, t, p, rows].astype(F32), W[g, t + 2, p, rows].astype(F32)
                left = jnp.where(lane > 0, pltpu.roll(u, 1, axis=1), 0.0)
                right = jnp.where(lane < 127, pltpu.roll(u, 127, axis=1), 0.0)
                sb[g, t, rows, p * 128:p * 128 + 128] = (0.5 * (right - left)).astype(BF16)
                sb[g, t, rows, 256 + p * 128:256 + p * 128 + 128] = (0.5 * (after - before)).astype(BF16)

            @pl.when(j < 4)
            def _():
                field_copy(i, j, 0).start()

            return carry

        lax.fori_loop(1, 5, step, 0)

    def x_slopes(i):
        g, lo, n = PIECES[i]
        rows = slice(lo, lo + n)

        def step(j, carry):
            t = lax.rem(x + j, 4)
            u0, u1 = W[g, t + 1, 0, rows].astype(F32), W[g, t + 1, 1, rows].astype(F32)
            low, high = H[g, 0, t, rows].astype(F32), H[g, 1, t, rows].astype(F32)
            sb[g, t, rows, 512:640] = (0.5 * (u1 - low)).astype(BF16)
            sb[g, t, rows, 640:768] = (0.5 * (high - u0)).astype(BF16)

            @pl.when(j < 4)
            def _():
                field_copy(i, j, 1).start()

            return carry

        lax.fori_loop(1, 5, step, 0)
        S[electrodes(i, group(i)), :] = sb[g, x, rows]

    def forward(i, d):
        origin = (zh if PIECES[i][0] == 0 else 1 - zh) * 8 + lax.rem(x + 4 - d, 4) * 2 + c
        rows = electrodes(i, origin)
        return remote(S.at[rows], S.at[rows], ws.at[i, d], wr.at[i, d], other_core)

    def slab(a, b):
        return pl.ds(pl.multiple_of((a * 4 + b) * ROWS, 16), ROWS)

    wide_b = pl.ds(pl.multiple_of(x * 4 * ROWS, 16), 4 * ROWS)

    def slab_copies(d):
        a, b = Tb.at[0:NA, slab(y, x)], Tb.at[NA:8, slab(x, y)]
        return (remote(a, a, p2_s.at[0, d - 1], p2_r.at[0, d - 1], x_peer(d)),
                remote(b, b, p2_s.at[1, d - 1], p2_r.at[1, d - 1], y_peer(d)))

    def wide_copy(d, dy):
        a = Tb.at[0:NA, slab(y, lax.rem(x + 4 - d, 4))]
        return remote(a, a, p3_s.at[d, dy - 1], p3_r.at[d, dy - 1], y_peer(dy))

    def wide_copy_b(d):
        b = Tb.at[NA:8, wide_b]
        return remote(b, b, p4_s.at[d - 1], p4_r.at[d - 1], x_peer(d))

    def pass_on(i, d):
        field_copy(i, d, 0).wait_recv()
        field_copy(i, d, 1).wait_recv()
        forward(i, d).start()

    def start_all(copies):
        for copy in copies:
            copy.start()

    def arrived(copies):
        for copy in copies:
            copy.wait_recv()

    arrived(z_copy(d) for d in range(1, 8))
    raw_copy(1).start()
    raw_copy(2).start()
    for d in range(1, 4):
        start_all(slab_copies(d))
    start_all(wide_copy(0, dy) for dy in (1, 3, 2))
    zy_slopes(0)
    halo_arrived(0)
    x_slopes(0)
    forward(0, 0).start()
    for d in (1, 3, 2):
        arrived(slab_copies(d))
        start_all(wide_copy(d, dy) for dy in (1, 3, 2))
    start_all(wide_copy_b(d) for d in (1, 3, 2))
    raw_copy(1).wait_recv()
    start_halo(1)
    zy_slopes(1)
    halo_arrived(1)
    x_slopes(1)
    forward(1, 0).start()
    raw_copy(2).wait_recv()
    start_halo(2)
    zy_slopes(2)
    for d in (1, 3, 2):
        pass_on(0, d)
    halo_arrived(2)
    x_slopes(2)
    forward(2, 0).start()
    for i in (1, 2):
        for d in (1, 3, 2):
            pass_on(i, d)
    for i in range(3):
        arrived(forward(i, d) for d in range(4))

    def product(jj, k, acc):
        rows = pl.ds(pl.multiple_of(k * 4 * ROWS, 16), 4 * ROWS)
        lhs = jnp.concatenate([Tb[2 * jj, rows], Tb[2 * jj + 1, rows]], axis=1)
        first = (c * 4 + jj) * 256
        for n in range(3):
            cols = slice(n * 256, n * 256 + 256)
            image = jnp.dot(lhs, S[pl.ds(pl.multiple_of(first, 256), 256), cols], preferred_element_type=F32)
            for b in range(5):
                own_rows = pl.ds(pl.multiple_of((first + k * 4 * ROWS + b * 64) & (E - 1), 64), 64)
                prod = image[b * 64:b * 64 + 64] * S[own_rows, cols].astype(F32)
                acc = acc + jnp.sum(prod.reshape(8, 8, 256), axis=0)
        return acc

    total = jnp.zeros((8, 256), F32)
    for d in (0, 1, 3, 2):
        if d > 0:
            arrived(wide_copy(o, d) for o in range(4))
        total = lax.fori_loop(0, NA // 2, lambda jj, acc: product(jj, lax.rem(y + 4 - d, 4), acc), total)
    for d in (0, 1, 3, 2) if NA < 8 else ():
        if d > 0:
            wide_copy_b(d).wait_recv()
        total = lax.fori_loop(NA // 2, 4, lambda jj, acc: product(jj, lax.rem(x + 4 - d, 4), acc), total)
    total = jnp.sum(total, axis=0, keepdims=True)
    gs[...] = jnp.zeros((8, 128), F32)
    gs[0:1, :] = total[:, 0:128]
    gs[1:2, :] = total[:, 128:256]

    def share(k):
        return remote(gs, gr.at[e], g_s.at[k - 1], g_r.at[k - 1], elec_peer(k))

    for k in range(1, 16):
        share(k).start()
    gr[e] = gs[...]
    for k in range(1, 16):
        share(k).wait_recv()
    for m in range(8):
        both = gr[2 * m] + gr[2 * m + 1]
        for p in range(2):
            out[p, m:m + 1, :] = both[p:p + 1, :] * weight[p, m:m + 1, :]


    sent = [raw_copy(1), raw_copy(2)]
    for i in range(3):
        halo_sent(i)
        sent += [field_copy(i, d, part) for d in range(1, 4) for part in range(2)]
        sent += [forward(i, d) for d in range(4)]
    sent += [z_copy(d) for d in range(1, 8)]
    for d in range(1, 4):
        sent += slab_copies(d)
        sent += [wide_copy(o, d) for o in range(4)]
        sent += [wide_copy_b(d)]
    sent += [share(k) for k in range(1, 16)]
    for copy in sent:
        copy.wait_send()


def local(potentials, quadrupoles, residuals, cell_weight):
    dma = pltpu.SemaphoreType.DMA
    return pl.pallas_call(
        kernel,
        name="misfit_gradient",
        out_shape=jax.ShapeDtypeStruct(cell_weight.shape, F32),
        in_specs=[pl.BlockSpec(memory_space=pltpu.VMEM)] * 4,
        out_specs=pl.BlockSpec(memory_space=pltpu.VMEM),
        scratch_shapes=[
            pltpu.VMEM((EL * 16, 128), F32),
            pltpu.VMEM((2, 6, 2, EL, 128), BF16),
            pltpu.VMEM((6, 2, EL, 128), BF16),
            pltpu.VMEM((2, 2, 4, EL, 128), BF16),
            pltpu.VMEM((2, 4, EL, NC), BF16),
            pltpu.VMEM((E, NC), BF16),
            pltpu.VMEM((8, WIN, 128), BF16),
            pltpu.VMEM((8, 128), F32),
            pltpu.VMEM((16, 8, 128), F32),
            dma((2,)), dma((2,)),
            dma((3, 2)), dma((3, 2)),
            dma((3, 2, 3)), dma((3, 2, 3)),
            dma((3, 4)), dma((3, 4)),
            dma((7,)), dma((7,)),
            dma((2, 3)), dma((2, 3)),
            dma((4, 3)), dma((4, 3)),
            dma((3,)), dma((3,)),
            dma((15,)), dma((15,)),
        ],
        compiler_params=pltpu.CompilerParams(
            collective_id=0, has_side_effects=True, vmem_limit_bytes=56 << 20),
    )(potentials, quadrupoles, residuals.reshape(1, QUADS), cell_weight)


def solution(mesh):
    placed = (P("elec", "space", None, None), P(), P(), P("space", None, None))
    return jax.shard_map(
        local, mesh=mesh, in_specs=placed, out_specs=P("space", None, None), check_vma=False
    )
```

```python
import jax
import jax.numpy as jnp
from jax import lax
from jax.experimental import pallas as pl
from jax.experimental.pallas import tpu as pltpu
from jax.sharding import PartitionSpec as P

MESH = pl.DeviceIdType.MESH
F32 = jnp.float32
BF16 = jnp.bfloat16
E = 2048
EL = 128
QUADS = 32768
QK = 4096
ROWS = 80
WIN = 1280
PIECES = ((0, 0, 128), (1, 0, 64), (1, 64, 64))
NC = 768


def kernel(pot, quad, res, weight, out,
           uf, W, sr, H, sb, S, Tb, gs, gx, gt, gr,
           r_s, r_r, halo_s, halo_r, fs, fr, ws, wr, z_s, z_r, p2_s, p2_r, p3_s, p3_r, p4_s, p4_r, c_s, c_r, g_s, g_r):
    e = lax.axis_index("elec")
    s = lax.axis_index("space")
    zh, x, c = e // 8, (e // 2) % 4, e % 2
    zl, y = s // 4, s % 4
    z = zh * 4 + zl
    mi = zh * 4 + x

    def chip_peer(k):
        return (lax.rem(mi + k, 8) * 2 + c, s)

    def space_peer(d):
        return (e, lax.rem(s + d + 16, 16))

    def z_peer(d):
        t = lax.rem(z + d, 8)
        return ((t // 4) * 8 + x * 2 + c, lax.rem(t, 4) * 4 + y)

    def x_peer(d):
        return (zh * 8 + lax.rem(x + d, 4) * 2 + c, s)

    def y_peer(d):
        return (e, zl * 4 + lax.rem(y + d, 4))

    other_core = (zh * 8 + x * 2 + (1 - c), s)
    partner = lax.rem(e + 8, 16)

    def remote(src, dst, ss, rs, device):
        return pltpu.make_async_remote_copy(
            src_ref=src, dst_ref=dst, send_sem=ss, recv_sem=rs, device_id=device, device_id_type=MESH)

    barrier = pltpu.get_barrier_semaphore()
    peers = ([chip_peer(k) for k in range(1, 8)] + [other_core, space_peer(1), space_peer(-1)]
             + [z_peer(d) for d in (1, 2, 3, 5, 6, 7)] + [y_peer(d) for d in (1, 2, 3)])
    for peer in peers:
        pl.semaphore_signal(barrier, inc=1, device_id=peer, device_id_type=MESH)

    rb = y * 4 + x
    col0 = c * 1024 + z * 128
    row0 = (c * 4 + z // 2) * 256 + rb * ROWS
    row_ids = ((lax.broadcasted_iota(jnp.int32, (ROWS, QK), 0) + row0) & (E - 1)).astype(jnp.int16)
    col_ids = (lax.broadcasted_iota(jnp.int32, (EL, QK), 0) + col0).astype(jnp.int16)
    one = jnp.ones((16, QK), BF16)
    zero = jnp.zeros((16, QK), BF16)

    def hot(u, v, ids, plus, minus):
        return jnp.concatenate(
            [jnp.where(u == ids[k:k + 16], plus, jnp.where(v == ids[k:k + 16], minus, zero))
             for k in range(0, ids.shape[0], 16)], axis=0)

    def nt(a, b):
        return lax.dot_general(a, b, (((1,), (1,)), ((), ())), preferred_element_type=F32)

    def quad_step(i, acc):
        q = pl.ds(pl.multiple_of(i * QK, QK), QK)
        a, b, m, n = (quad[k:k + 1, q] for k in range(4))
        r = jnp.where((a == b) | (m == n), 0.0, res[0:1, q])
        a, b, m, n = (jnp.broadcast_to(v, (16, QK)).astype(jnp.int16) for v in (a, b, m, n))
        r = jnp.broadcast_to(r, (16, QK)).astype(BF16)
        acc = acc + nt(hot(a, b, row_ids, one, -one), hot(m, n, col_ids, r, -r))
        return acc + nt(hot(m, n, row_ids, one, -one), hot(a, b, col_ids, r, -r))

    block = lax.fori_loop(0, QUADS // QK, quad_step, jnp.zeros((ROWS, EL), F32))
    offset = lax.broadcasted_iota(jnp.int32, (ROWS, EL), 0) + rb * ROWS
    block = jnp.where((offset < 256) | (offset >= 1024), 0.5 * block, block)
    own = pl.ds(pl.multiple_of(rb * ROWS, 16), ROWS)
    Tb[z, own, :] = block.astype(BF16)

    pl.semaphore_wait(barrier, len(peers))

    raw = pl.ds(zh, 5)

    def raw_copy(i):
        _, lo, n = PIECES[i]
        return remote(sr.at[raw, :, lo:lo + n], W.at[1, raw, :, lo:lo + n], r_s.at[i - 1], r_r.at[i - 1], (partner, s))

    def halo_copies(i):
        g, lo, n = PIECES[i]
        return (remote(W.at[g, 1:5, 1, lo:lo + n], H.at[g, 0, :, lo:lo + n],
                       halo_s.at[i, 0], halo_r.at[i, 0], space_peer(1)),
                remote(W.at[g, 1:5, 0, lo:lo + n], H.at[g, 1, :, lo:lo + n],
                       halo_s.at[i, 1], halo_r.at[i, 1], space_peer(-1)))

    def start_halo(i):
        up, down = halo_copies(i)

        @pl.when(s < 15)
        def _():
            up.start()

        @pl.when(s > 0)
        def _():
            down.start()

    def halo_arrived(i):
        up, down = halo_copies(i)

        @pl.when(s > 0)
        def _():
            up.wait_recv()

        @pl.when(s < 15)
        def _():
            down.wait_recv()

    def halo_sent(i):
        up, down = halo_copies(i)

        @pl.when(s < 15)
        def _():
            up.wait_send()

        @pl.when(s > 0)
        def _():
            down.wait_send()

    def z_copy(d):
        return remote(Tb.at[z, own], Tb.at[z, own], z_s.at[d - 1], z_r.at[d - 1], z_peer(d))

    for d in range(1, 8):
        z_copy(d).start()
    uf[...] = pot[...].astype(F32).reshape(EL * 16, 128)

    def half_step(i, carry):
        for p in range(2):
            mine = zh * 4 + i - 1
            u = uf[pl.ds(p * 8 + jnp.clip(mine, 0, 7), EL, stride=16), :]
            W[0, i, p] = jnp.where((mine >= 0) & (mine < 8), u, 0.0).astype(BF16)
            theirs = (1 - zh) * 4 + i - 1
            sr[i, p] = uf[pl.ds(p * 8 + jnp.clip(theirs, 0, 7), EL, stride=16), :].astype(BF16)
        return carry

    lax.fori_loop(0, 6, half_step, 0)
    W[1, 5 * zh] = jnp.zeros((2, EL, 128), BF16)

    @pl.when(s == 0)
    def _():
        H[:, 0] = jnp.zeros((2, 4, EL, 128), BF16)

    @pl.when(s == 15)
    def _():
        H[:, 1] = jnp.zeros((2, 4, EL, 128), BF16)

    start_halo(0)
    def electrodes(i, origin):
        _, lo, n = PIECES[i]
        return pl.ds(pl.multiple_of(origin * EL + lo, 64), n)

    def group(i):
        return e if PIECES[i][0] == 0 else partner

    def field_copy(i, d, part):
        g, lo, n = PIECES[i]
        tx = lax.rem(x + d, 4)
        cols = pl.ds(0, 512) if part == 0 else pl.ds(512, 256)
        return remote(sb.at[g, tx, lo:lo + n, cols], S.at[electrodes(i, group(i)), cols],
                      fs.at[i, part, d - 1], fr.at[i, part, d - 1], x_peer(d))

    def zy_slopes(i):
        g, lo, n = PIECES[i]
        rows = slice(lo, lo + n)
        lane = lax.broadcasted_iota(jnp.int32, (n, 128), 1)

        def step(j, carry):
            t = lax.rem(x + j, 4)
            for p in range(2):
                u = W[g, t + 1, p, rows].astype(F32)
                before, after = W[g, t, p, rows].astype(F32), W[g, t + 2, p, rows].astype(F32)
                left = jnp.where(lane > 0, pltpu.roll(u, 1, axis=1), 0.0)
                right = jnp.where(lane < 127, pltpu.roll(u, 127, axis=1), 0.0)
                sb[g, t, rows, p * 128:p * 128 + 128] = (0.5 * (right - left)).astype(BF16)
                sb[g, t, rows, 256 + p * 128:256 + p * 128 + 128] = (0.5 * (after - before)).astype(BF16)

            @pl.when(j < 4)
            def _():
                field_copy(i, j, 0).start()

            return carry

        lax.fori_loop(1, 5, step, 0)

    def x_slopes(i):
        g, lo, n = PIECES[i]
        rows = slice(lo, lo + n)

        def step(j, carry):
            t = lax.rem(x + j, 4)
            u0, u1 = W[g, t + 1, 0, rows].astype(F32), W[g, t + 1, 1, rows].astype(F32)
            low, high = H[g, 0, t, rows].astype(F32), H[g, 1, t, rows].astype(F32)
            sb[g, t, rows, 512:640] = (0.5 * (u1 - low)).astype(BF16)
            sb[g, t, rows, 640:768] = (0.5 * (high - u0)).astype(BF16)

            @pl.when(j < 4)
            def _():
                field_copy(i, j, 1).start()

            return carry

        lax.fori_loop(1, 5, step, 0)
        S[electrodes(i, group(i)), :] = sb[g, x, rows]

    def forward(i, d):
        origin = (zh if PIECES[i][0] == 0 else 1 - zh) * 8 + lax.rem(x + 4 - d, 4) * 2 + c
        rows = electrodes(i, origin)
        return remote(S.at[rows], S.at[rows], ws.at[i, d], wr.at[i, d], other_core)

    def slab(a, b):
        return pl.ds(pl.multiple_of((a * 4 + b) * ROWS, 16), ROWS)

    def slab_copy(d):
        a = Tb.at[:, slab(y, x)]
        return remote(a, a, p2_s.at[d - 1], p2_r.at[d - 1], x_peer(d))

    def wide_copy(d, dy):
        a = Tb.at[:, slab(y, lax.rem(x + 4 - d, 4))]
        return remote(a, a, p3_s.at[d, dy - 1], p3_r.at[d, dy - 1], y_peer(dy))

    def relay_copy(d, half):
        a = Tb.at[half * 4:half * 4 + 4, slab(lax.rem(y + (3, 1)[half], 4), lax.rem(x + 4 - d, 4))]
        return remote(a, a, p4_s.at[d, half], p4_r.at[d, half], y_peer((1, 3)[half]))

    def relay(d):
        for half, dy in ((0, 1), (1, 3)):
            wide_copy(d, dy).wait_recv()
            relay_copy(d, half).start()

    def pass_on(i, d):
        field_copy(i, d, 0).wait_recv()
        field_copy(i, d, 1).wait_recv()
        forward(i, d).start()

    def start_all(copies):
        for copy in copies:
            copy.start()

    def arrived(copies):
        for copy in copies:
            copy.wait_recv()

    arrived(z_copy(d) for d in range(1, 8))
    raw_copy(1).start()
    raw_copy(2).start()
    start_all(slab_copy(d) for d in (1, 3, 2))
    zy_slopes(0)
    halo_arrived(0)
    x_slopes(0)
    forward(0, 0).start()
    start_all(wide_copy(0, dy) for dy in (1, 3))
    slab_copy(1).wait_recv()
    start_all(wide_copy(1, dy) for dy in (1, 3))
    raw_copy(1).wait_recv()
    start_halo(1)
    zy_slopes(1)
    relay(0)
    slab_copy(3).wait_recv()
    start_all(wide_copy(3, dy) for dy in (1, 3))
    halo_arrived(1)
    x_slopes(1)
    forward(1, 0).start()
    relay(1)
    raw_copy(2).wait_recv()
    start_halo(2)
    zy_slopes(2)
    slab_copy(2).wait_recv()
    start_all(wide_copy(2, dy) for dy in (1, 3))
    halo_arrived(2)
    x_slopes(2)
    forward(2, 0).start()
    relay(3)
    for d in (1, 3, 2):
        pass_on(0, d)
    relay(2)
    for i in (1, 2):
        for d in (1, 3, 2):
            pass_on(i, d)
    for i in range(3):
        arrived(forward(i, d) for d in range(4))

    def product(jj, k, acc):
        rows = pl.ds(pl.multiple_of(k * 4 * ROWS, 16), 4 * ROWS)
        lhs = jnp.concatenate([Tb[2 * jj, rows], Tb[2 * jj + 1, rows]], axis=1)
        first = (c * 4 + jj) * 256
        for n in range(3):
            cols = slice(n * 256, n * 256 + 256)
            image = jnp.dot(lhs, S[pl.ds(pl.multiple_of(first, 256), 256), cols], preferred_element_type=F32)
            for b in range(5):
                own_rows = pl.ds(pl.multiple_of((first + k * 4 * ROWS + b * 64) & (E - 1), 64), 64)
                prod = image[b * 64:b * 64 + 64] * S[own_rows, cols].astype(F32)
                acc = acc + jnp.sum(prod.reshape(8, 8, 256), axis=0)
        return acc

    total = jnp.zeros((8, 256), F32)
    for d in (0, 1, 3, 2):
        if d == 2:
            arrived(relay_copy(o, half) for o in range(4) for half in range(2))
        total = lax.fori_loop(0, 4, lambda jj, acc: product(jj, lax.rem(y + 4 - d, 4), acc), total)
    total = jnp.sum(total, axis=0, keepdims=True)
    gs[...] = jnp.zeros((8, 128), F32)
    gs[0:1, :] = total[:, 0:128]
    gs[1:2, :] = total[:, 128:256]

    cores = remote(gs, gx, c_s, c_r, other_core)
    cores.start()
    cores.wait_recv()
    gt[...] = gs[...] + gx[...]

    def share(k):
        return remote(gt, gr.at[mi], g_s.at[k - 1], g_r.at[k - 1], chip_peer(k))

    for k in range(1, 8):
        share(k).start()
    gr[mi] = gt[...]
    for k in range(1, 8):
        share(k).wait_recv()
    for m in range(8):
        for p in range(2):
            out[p, m:m + 1, :] = gr[m, p:p + 1, :] * weight[p, m:m + 1, :]

    sent = [raw_copy(1), raw_copy(2)]
    for i in range(3):
        halo_sent(i)
        sent += [field_copy(i, d, part) for d in range(1, 4) for part in range(2)]
        sent += [forward(i, d) for d in range(4)]
    sent += [z_copy(d) for d in range(1, 8)]
    for d in range(1, 4):
        sent += [slab_copy(d)]
    for o in range(4):
        sent += [wide_copy(o, dy) for dy in (1, 3)] + [relay_copy(o, half) for half in range(2)]
    sent += [cores] + [share(k) for k in range(1, 8)]
    for copy in sent:
        copy.wait_send()


def local(potentials, quadrupoles, residuals, cell_weight):
    dma = pltpu.SemaphoreType.DMA
    return pl.pallas_call(
        kernel,
        name="misfit_gradient",
        out_shape=jax.ShapeDtypeStruct(cell_weight.shape, F32),
        in_specs=[pl.BlockSpec(memory_space=pltpu.VMEM)] * 4,
        out_specs=pl.BlockSpec(memory_space=pltpu.VMEM),
        scratch_shapes=[
            pltpu.VMEM((EL * 16, 128), F32),
            pltpu.VMEM((2, 6, 2, EL, 128), BF16),
            pltpu.VMEM((6, 2, EL, 128), BF16),
            pltpu.VMEM((2, 2, 4, EL, 128), BF16),
            pltpu.VMEM((2, 4, EL, NC), BF16),
            pltpu.VMEM((E, NC), BF16),
            pltpu.VMEM((8, WIN, 128), BF16),
            pltpu.VMEM((8, 128), F32),
            pltpu.VMEM((8, 128), F32),
            pltpu.VMEM((8, 128), F32),
            pltpu.VMEM((8, 8, 128), F32),
            dma((2,)), dma((2,)),
            dma((3, 2)), dma((3, 2)),
            dma((3, 2, 3)), dma((3, 2, 3)),
            dma((3, 4)), dma((3, 4)),
            dma((7,)), dma((7,)),
            dma((3,)), dma((3,)),
            dma((4, 3)), dma((4, 3)),
            dma((4, 2)), dma((4, 2)),
            dma(()), dma(()),
            dma((7,)), dma((7,)),
        ],
        compiler_params=pltpu.CompilerParams(
            collective_id=0, has_side_effects=True, vmem_limit_bytes=56 << 20),
    )(potentials, quadrupoles, residuals.reshape(1, QUADS), cell_weight)


def solution(mesh):
    placed = (P("elec", "space", None, None), P(), P(), P("space", None, None))
    return jax.shard_map(
        local, mesh=mesh, in_specs=placed, out_specs=P("space", None, None), check_vma=False
    )
```

```python
import jax
import jax.numpy as jnp
from jax import lax
from jax.experimental import pallas as pl
from jax.experimental.pallas import tpu as pltpu
from jax.sharding import PartitionSpec as P

MESH = pl.DeviceIdType.MESH
F32 = jnp.float32
BF16 = jnp.bfloat16
E = 2048
EL = 128
QUADS = 32768
QK = 4096
ROWS = 80
WIN = 1280
PIECES = ((0, 0, 128), (1, 0, 64), (1, 64, 64))
NC = 768


def kernel(pot, quad, res, weight, out,
           uf, W, sr, H, sb, S, Tb, gs, gx, gt, gr,
           r_s, r_r, halo_s, halo_r, fs, fr, ws, wr, z_s, z_r, p2_s, p2_r, p3_s, p3_r, p4_s, p4_r, c_s, c_r, g_s, g_r):
    e = lax.axis_index("elec")
    s = lax.axis_index("space")
    zh, x, c = e // 8, (e // 2) % 4, e % 2
    zl, y = s // 4, s % 4
    z = zh * 4 + zl
    mi = zh * 4 + x

    def chip_peer(k):
        return (lax.rem(mi + k, 8) * 2 + c, s)

    def space_peer(d):
        return (e, lax.rem(s + d + 16, 16))

    def z_peer(d):
        t = lax.rem(z + d, 8)
        return ((t // 4) * 8 + x * 2 + c, lax.rem(t, 4) * 4 + y)

    def x_peer(d):
        return (zh * 8 + lax.rem(x + d, 4) * 2 + c, s)

    def y_peer(d):
        return (e, zl * 4 + lax.rem(y + d, 4))

    other_core = (zh * 8 + x * 2 + (1 - c), s)
    partner = lax.rem(e + 8, 16)

    def remote(src, dst, ss, rs, device):
        return pltpu.make_async_remote_copy(
            src_ref=src, dst_ref=dst, send_sem=ss, recv_sem=rs, device_id=device, device_id_type=MESH)

    barrier = pltpu.get_barrier_semaphore()
    peers = ([chip_peer(k) for k in range(1, 8)] + [other_core, space_peer(1), space_peer(-1)]
             + [z_peer(d) for d in (1, 2, 3, 5, 6, 7)] + [y_peer(d) for d in (1, 2, 3)])
    for peer in peers:
        pl.semaphore_signal(barrier, inc=1, device_id=peer, device_id_type=MESH)

    rb = y * 4 + x
    col0 = c * 1024 + z * 128
    row0 = (c * 4 + z // 2) * 256 + rb * ROWS
    row_ids = ((lax.broadcasted_iota(jnp.int32, (ROWS, QK), 0) + row0) & (E - 1)).astype(jnp.int16)
    col_ids = (lax.broadcasted_iota(jnp.int32, (EL, QK), 0) + col0).astype(jnp.int16)
    one = jnp.ones((16, QK), BF16)
    zero = jnp.zeros((16, QK), BF16)

    def hot(u, v, ids, plus, minus):
        return jnp.concatenate(
            [jnp.where(u == ids[k:k + 16], plus, jnp.where(v == ids[k:k + 16], minus, zero))
             for k in range(0, ids.shape[0], 16)], axis=0)

    def nt(a, b):
        return lax.dot_general(a, b, (((1,), (1,)), ((), ())), preferred_element_type=F32)

    def quad_step(i, acc):
        q = pl.ds(pl.multiple_of(i * QK, QK), QK)
        a, b, m, n = (quad[k:k + 1, q] for k in range(4))
        r = jnp.where((a == b) | (m == n), 0.0, res[0:1, q])
        a, b, m, n = (jnp.broadcast_to(v, (16, QK)).astype(jnp.int16) for v in (a, b, m, n))
        r = jnp.broadcast_to(r, (16, QK)).astype(BF16)
        acc = acc + nt(hot(a, b, row_ids, one, -one), hot(m, n, col_ids, r, -r))
        return acc + nt(hot(m, n, row_ids, one, -one), hot(a, b, col_ids, r, -r))

    block = lax.fori_loop(0, QUADS // QK, quad_step, jnp.zeros((ROWS, EL), F32))
    offset = lax.broadcasted_iota(jnp.int32, (ROWS, EL), 0) + rb * ROWS
    block = jnp.where((offset < 256) | (offset >= 1024), 0.5 * block, block)
    own = pl.ds(pl.multiple_of(rb * ROWS, 16), ROWS)
    Tb[z, own, :] = block.astype(BF16)

    pl.semaphore_wait(barrier, len(peers))

    raw = pl.ds(zh, 5)

    def raw_copy(i):
        _, lo, n = PIECES[i]
        return remote(sr.at[raw, :, lo:lo + n], W.at[1, raw, :, lo:lo + n], r_s.at[i - 1], r_r.at[i - 1], (partner, s))

    def halo_copies(i):
        g, lo, n = PIECES[i]
        return (remote(W.at[g, 1:5, 1, lo:lo + n], H.at[g, 0, :, lo:lo + n],
                       halo_s.at[i, 0], halo_r.at[i, 0], space_peer(1)),
                remote(W.at[g, 1:5, 0, lo:lo + n], H.at[g, 1, :, lo:lo + n],
                       halo_s.at[i, 1], halo_r.at[i, 1], space_peer(-1)))

    def start_halo(i):
        up, down = halo_copies(i)

        @pl.when(s < 15)
        def _():
            up.start()

        @pl.when(s > 0)
        def _():
            down.start()

    def halo_arrived(i):
        up, down = halo_copies(i)

        @pl.when(s > 0)
        def _():
            up.wait_recv()

        @pl.when(s < 15)
        def _():
            down.wait_recv()

    def halo_sent(i):
        up, down = halo_copies(i)

        @pl.when(s < 15)
        def _():
            up.wait_send()

        @pl.when(s > 0)
        def _():
            down.wait_send()

    def z_copy(d):
        return remote(Tb.at[z, own], Tb.at[z, own], z_s.at[d - 1], z_r.at[d - 1], z_peer(d))

    for d in (4, 3, 5, 2, 6, 1, 7):
        z_copy(d).start()
    uf[...] = pot[...].astype(F32).reshape(EL * 16, 128)

    def half_step(i, carry):
        for p in range(2):
            mine = zh * 4 + i - 1
            u = uf[pl.ds(p * 8 + jnp.clip(mine, 0, 7), EL, stride=16), :]
            W[0, i, p] = jnp.where((mine >= 0) & (mine < 8), u, 0.0).astype(BF16)
            theirs = (1 - zh) * 4 + i - 1
            sr[i, p] = uf[pl.ds(p * 8 + jnp.clip(theirs, 0, 7), EL, stride=16), :].astype(BF16)
        return carry

    lax.fori_loop(0, 6, half_step, 0)
    W[1, 5 * zh] = jnp.zeros((2, EL, 128), BF16)

    @pl.when(s == 0)
    def _():
        H[:, 0] = jnp.zeros((2, 4, EL, 128), BF16)

    @pl.when(s == 15)
    def _():
        H[:, 1] = jnp.zeros((2, 4, EL, 128), BF16)

    start_halo(0)
    def electrodes(i, origin):
        _, lo, n = PIECES[i]
        return pl.ds(pl.multiple_of(origin * EL + lo, 64), n)

    def group(i):
        return e if PIECES[i][0] == 0 else partner

    def field_copy(i, d, part):
        g, lo, n = PIECES[i]
        tx = lax.rem(x + d, 4)
        cols = pl.ds(0, 512) if part == 0 else pl.ds(512, 256)
        return remote(sb.at[g, tx, lo:lo + n, cols], S.at[electrodes(i, group(i)), cols],
                      fs.at[i, part, d - 1], fr.at[i, part, d - 1], x_peer(d))

    def zy_slopes(i):
        g, lo, n = PIECES[i]
        rows = slice(lo, lo + n)
        lane = lax.broadcasted_iota(jnp.int32, (n, 128), 1)

        def step(j, carry):
            t = lax.rem(x + j, 4)
            for p in range(2):
                u = W[g, t + 1, p, rows].astype(F32)
                before, after = W[g, t, p, rows].astype(F32), W[g, t + 2, p, rows].astype(F32)
                left = jnp.where(lane > 0, pltpu.roll(u, 1, axis=1), 0.0)
                right = jnp.where(lane < 127, pltpu.roll(u, 127, axis=1), 0.0)
                sb[g, t, rows, p * 128:p * 128 + 128] = (0.5 * (right - left)).astype(BF16)
                sb[g, t, rows, 256 + p * 128:256 + p * 128 + 128] = (0.5 * (after - before)).astype(BF16)

            @pl.when(j < 4)
            def _():
                field_copy(i, j, 0).start()

            return carry

        lax.fori_loop(1, 5, step, 0)

    def x_slopes(i):
        g, lo, n = PIECES[i]
        rows = slice(lo, lo + n)

        def step(j, carry):
            t = lax.rem(x + j, 4)
            u0, u1 = W[g, t + 1, 0, rows].astype(F32), W[g, t + 1, 1, rows].astype(F32)
            low, high = H[g, 0, t, rows].astype(F32), H[g, 1, t, rows].astype(F32)
            sb[g, t, rows, 512:640] = (0.5 * (u1 - low)).astype(BF16)
            sb[g, t, rows, 640:768] = (0.5 * (high - u0)).astype(BF16)

            @pl.when(j < 4)
            def _():
                field_copy(i, j, 1).start()

            return carry

        lax.fori_loop(1, 5, step, 0)
        S[electrodes(i, group(i)), :] = sb[g, x, rows]

    def forward(i, d):
        origin = (zh if PIECES[i][0] == 0 else 1 - zh) * 8 + lax.rem(x + 4 - d, 4) * 2 + c
        rows = electrodes(i, origin)
        return remote(S.at[rows], S.at[rows], ws.at[i, d], wr.at[i, d], other_core)

    def slab(a, b):
        return pl.ds(pl.multiple_of((a * 4 + b) * ROWS, 16), ROWS)

    def slab_copy(d):
        a = Tb.at[:, slab(y, x)]
        return remote(a, a, p2_s.at[d - 1], p2_r.at[d - 1], x_peer(d))

    def wide_copy(d, dy):
        a = Tb.at[:, slab(y, lax.rem(x + 4 - d, 4))]
        return remote(a, a, p3_s.at[d, dy - 1], p3_r.at[d, dy - 1], y_peer(dy))

    def relay_copy(d, half):
        a = Tb.at[half * 4:half * 4 + 4, slab(lax.rem(y + (3, 1)[half], 4), lax.rem(x + 4 - d, 4))]
        return remote(a, a, p4_s.at[d, half], p4_r.at[d, half], y_peer((1, 3)[half]))

    def relay(d):
        for half, dy in ((0, 1), (1, 3)):
            wide_copy(d, dy).wait_recv()
            relay_copy(d, half).start()

    def pass_on(i, d):
        field_copy(i, d, 0).wait_recv()
        field_copy(i, d, 1).wait_recv()
        forward(i, d).start()

    def start_all(copies):
        for copy in copies:
            copy.start()

    def arrived(copies):
        for copy in copies:
            copy.wait_recv()

    arrived(z_copy(d) for d in range(1, 8))
    raw_copy(1).start()
    raw_copy(2).start()
    start_all(slab_copy(d) for d in (1, 3, 2))
    start_all(wide_copy(0, dy) for dy in (1, 3))
    zy_slopes(0)
    halo_arrived(0)
    x_slopes(0)
    forward(0, 0).start()
    slab_copy(1).wait_recv()
    start_all(wide_copy(1, dy) for dy in (1, 3))
    raw_copy(1).wait_recv()
    start_halo(1)
    zy_slopes(1)
    slab_copy(3).wait_recv()
    start_all(wide_copy(3, dy) for dy in (1, 3))
    relay(0)
    halo_arrived(1)
    x_slopes(1)
    forward(1, 0).start()
    raw_copy(2).wait_recv()
    start_halo(2)
    zy_slopes(2)
    relay(1)
    slab_copy(2).wait_recv()
    start_all(wide_copy(2, dy) for dy in (1, 3))
    halo_arrived(2)
    x_slopes(2)
    forward(2, 0).start()
    relay(3)
    for d in (1, 3, 2):
        pass_on(0, d)
    relay(2)
    for i in (1, 2):
        for d in (1, 3, 2):
            pass_on(i, d)
    for i in range(3):
        arrived(forward(i, d) for d in range(4))

    def product(jj, k, acc):
        rows = pl.ds(pl.multiple_of(k * 4 * ROWS, 16), 4 * ROWS)
        lhs = jnp.concatenate([Tb[2 * jj, rows], Tb[2 * jj + 1, rows]], axis=1)
        first = (c * 4 + jj) * 256
        for n in range(3):
            cols = slice(n * 256, n * 256 + 256)
            image = jnp.dot(lhs, S[pl.ds(pl.multiple_of(first, 256), 256), cols], preferred_element_type=F32)
            for b in range(5):
                own_rows = pl.ds(pl.multiple_of((first + k * 4 * ROWS + b * 64) & (E - 1), 64), 64)
                prod = image[b * 64:b * 64 + 64] * S[own_rows, cols].astype(F32)
                acc = acc + jnp.sum(prod.reshape(8, 8, 256), axis=0)
        return acc

    total = jnp.zeros((8, 256), F32)
    for d in (0, 1, 3, 2):
        if d == 2:
            arrived(relay_copy(o, half) for o in range(4) for half in range(2))
        total = lax.fori_loop(0, 4, lambda jj, acc: product(jj, lax.rem(y + 4 - d, 4), acc), total)
    total = jnp.sum(total, axis=0, keepdims=True)
    gs[...] = jnp.zeros((8, 128), F32)
    gs[0:1, :] = total[:, 0:128]
    gs[1:2, :] = total[:, 128:256]

    cores = remote(gs, gx, c_s, c_r, other_core)
    cores.start()
    cores.wait_recv()
    gt[...] = gs[...] + gx[...]

    def share(k):
        return remote(gt, gr.at[mi], g_s.at[k - 1], g_r.at[k - 1], chip_peer(k))

    for k in (4, 3, 5, 2, 6, 1, 7):
        share(k).start()
    gr[mi] = gt[...]
    for k in range(1, 8):
        share(k).wait_recv()
    for m in range(8):
        for p in range(2):
            out[p, m:m + 1, :] = gr[m, p:p + 1, :] * weight[p, m:m + 1, :]

    sent = [raw_copy(1), raw_copy(2)]
    for i in range(3):
        halo_sent(i)
        sent += [field_copy(i, d, part) for d in range(1, 4) for part in range(2)]
        sent += [forward(i, d) for d in range(4)]
    sent += [z_copy(d) for d in range(1, 8)]
    for d in range(1, 4):
        sent += [slab_copy(d)]
    for o in range(4):
        sent += [wide_copy(o, dy) for dy in (1, 3)] + [relay_copy(o, half) for half in range(2)]
    sent += [cores] + [share(k) for k in range(1, 8)]
    for copy in sent:
        copy.wait_send()


def local(potentials, quadrupoles, residuals, cell_weight):
    dma = pltpu.SemaphoreType.DMA
    return pl.pallas_call(
        kernel,
        name="misfit_gradient",
        out_shape=jax.ShapeDtypeStruct(cell_weight.shape, F32),
        in_specs=[pl.BlockSpec(memory_space=pltpu.VMEM)] * 4,
        out_specs=pl.BlockSpec(memory_space=pltpu.VMEM),
        scratch_shapes=[
            pltpu.VMEM((EL * 16, 128), F32),
            pltpu.VMEM((2, 6, 2, EL, 128), BF16),
            pltpu.VMEM((6, 2, EL, 128), BF16),
            pltpu.VMEM((2, 2, 4, EL, 128), BF16),
            pltpu.VMEM((2, 4, EL, NC), BF16),
            pltpu.VMEM((E, NC), BF16),
            pltpu.VMEM((8, WIN, 128), BF16),
            pltpu.VMEM((8, 128), F32),
            pltpu.VMEM((8, 128), F32),
            pltpu.VMEM((8, 128), F32),
            pltpu.VMEM((8, 8, 128), F32),
            dma((2,)), dma((2,)),
            dma((3, 2)), dma((3, 2)),
            dma((3, 2, 3)), dma((3, 2, 3)),
            dma((3, 4)), dma((3, 4)),
            dma((7,)), dma((7,)),
            dma((3,)), dma((3,)),
            dma((4, 3)), dma((4, 3)),
            dma((4, 2)), dma((4, 2)),
            dma(()), dma(()),
            dma((7,)), dma((7,)),
        ],
        compiler_params=pltpu.CompilerParams(
            collective_id=0, has_side_effects=True, vmem_limit_bytes=56 << 20),
    )(potentials, quadrupoles, residuals.reshape(1, QUADS), cell_weight)


def solution(mesh):
    placed = (P("elec", "space", None, None), P(), P(), P("space", None, None))
    return jax.shard_map(
        local, mesh=mesh, in_specs=placed, out_specs=P("space", None, None), check_vma=False
    )
```

```python
import jax
import jax.numpy as jnp
from jax import lax
from jax.experimental import pallas as pl
from jax.experimental.pallas import tpu as pltpu
from jax.sharding import PartitionSpec as P

MESH = pl.DeviceIdType.MESH
F32 = jnp.float32
BF16 = jnp.bfloat16
E = 2048
EL = 128
QUADS = 32768
QK = 4096
ROWS = 80
WIN = 1280
PIECES = ((0, 0, 128), (1, 0, 128))
NC = 768


def kernel(pot, quad, res, weight, out,
           uf, W, sr, H, sb, S, Tb, gs, gx, gt, gr,
           r_s, r_r, halo_s, halo_r, fs, fr, ws, wr, z_s, z_r, p2_s, p2_r, p3_s, p3_r, p4_s, p4_r, c_s, c_r, g_s, g_r):
    e = lax.axis_index("elec")
    s = lax.axis_index("space")
    zh, x, c = e // 8, (e // 2) % 4, e % 2
    zl, y = s // 4, s % 4
    z = zh * 4 + zl
    mi = zh * 4 + x

    def chip_peer(k):
        return (lax.rem(mi + k, 8) * 2 + c, s)

    def space_peer(d):
        return (e, lax.rem(s + d + 16, 16))

    def z_peer(d):
        t = lax.rem(z + d, 8)
        return ((t // 4) * 8 + x * 2 + c, lax.rem(t, 4) * 4 + y)

    def x_peer(d):
        return (zh * 8 + lax.rem(x + d, 4) * 2 + c, s)

    def y_peer(d):
        return (e, zl * 4 + lax.rem(y + d, 4))

    other_core = (zh * 8 + x * 2 + (1 - c), s)
    partner = lax.rem(e + 8, 16)

    def remote(src, dst, ss, rs, device):
        return pltpu.make_async_remote_copy(
            src_ref=src, dst_ref=dst, send_sem=ss, recv_sem=rs, device_id=device, device_id_type=MESH)

    barrier = pltpu.get_barrier_semaphore()
    peers = ([chip_peer(k) for k in range(1, 8)] + [other_core, space_peer(1), space_peer(-1)]
             + [z_peer(d) for d in (1, 2, 3, 5, 6, 7)] + [y_peer(d) for d in (1, 2, 3)])
    for peer in peers:
        pl.semaphore_signal(barrier, inc=1, device_id=peer, device_id_type=MESH)

    rb = y * 4 + x
    col0 = c * 1024 + z * 128
    row0 = (c * 4 + z // 2) * 256 + rb * ROWS
    row_ids = ((lax.broadcasted_iota(jnp.int32, (ROWS, QK), 0) + row0) & (E - 1)).astype(jnp.int16)
    col_ids = (lax.broadcasted_iota(jnp.int32, (EL, QK), 0) + col0).astype(jnp.int16)
    one = jnp.ones((16, QK), BF16)
    zero = jnp.zeros((16, QK), BF16)

    def hot(u, v, ids, plus, minus):
        return jnp.concatenate(
            [jnp.where(u == ids[k:k + 16], plus, jnp.where(v == ids[k:k + 16], minus, zero))
             for k in range(0, ids.shape[0], 16)], axis=0)

    def nt(a, b):
        return lax.dot_general(a, b, (((1,), (1,)), ((), ())), preferred_element_type=F32)

    def quad_step(i, acc):
        q = pl.ds(pl.multiple_of(i * QK, QK), QK)
        a, b, m, n = (quad[k:k + 1, q] for k in range(4))
        r = jnp.where((a == b) | (m == n), 0.0, res[0:1, q])
        a, b, m, n = (jnp.broadcast_to(v, (16, QK)).astype(jnp.int16) for v in (a, b, m, n))
        r = jnp.broadcast_to(r, (16, QK)).astype(BF16)
        acc = acc + nt(hot(a, b, row_ids, one, -one), hot(m, n, col_ids, r, -r))
        return acc + nt(hot(m, n, row_ids, one, -one), hot(a, b, col_ids, r, -r))

    block = lax.fori_loop(0, QUADS // QK, quad_step, jnp.zeros((ROWS, EL), F32))
    offset = lax.broadcasted_iota(jnp.int32, (ROWS, EL), 0) + rb * ROWS
    block = jnp.where((offset < 256) | (offset >= 1024), 0.5 * block, block)
    own = pl.ds(pl.multiple_of(rb * ROWS, 16), ROWS)
    Tb[z, own, :] = block.astype(BF16)

    pl.semaphore_wait(barrier, len(peers))

    raw = pl.ds(zh, 5)

    def raw_copy(i):
        _, lo, n = PIECES[i]
        return remote(sr.at[raw, :, lo:lo + n], W.at[1, raw, :, lo:lo + n], r_s.at[i - 1], r_r.at[i - 1], (partner, s))

    def halo_copies(i):
        g, lo, n = PIECES[i]
        return (remote(W.at[g, 1:5, 1, lo:lo + n], H.at[g, 0, :, lo:lo + n],
                       halo_s.at[i, 0], halo_r.at[i, 0], space_peer(1)),
                remote(W.at[g, 1:5, 0, lo:lo + n], H.at[g, 1, :, lo:lo + n],
                       halo_s.at[i, 1], halo_r.at[i, 1], space_peer(-1)))

    def start_halo(i):
        up, down = halo_copies(i)

        @pl.when(s < 15)
        def _():
            up.start()

        @pl.when(s > 0)
        def _():
            down.start()

    def halo_arrived(i):
        up, down = halo_copies(i)

        @pl.when(s > 0)
        def _():
            up.wait_recv()

        @pl.when(s < 15)
        def _():
            down.wait_recv()

    def halo_sent(i):
        up, down = halo_copies(i)

        @pl.when(s < 15)
        def _():
            up.wait_send()

        @pl.when(s > 0)
        def _():
            down.wait_send()

    def z_copy(d):
        return remote(Tb.at[z, own], Tb.at[z, own], z_s.at[d - 1], z_r.at[d - 1], z_peer(d))

    for d in (4, 3, 5, 2, 6, 1, 7):
        z_copy(d).start()
    uf[...] = pot[...].astype(F32).reshape(EL * 16, 128)

    def half_step(i, carry):
        for p in range(2):
            mine = zh * 4 + i - 1
            u = uf[pl.ds(p * 8 + jnp.clip(mine, 0, 7), EL, stride=16), :]
            W[0, i, p] = jnp.where((mine >= 0) & (mine < 8), u, 0.0).astype(BF16)
            theirs = (1 - zh) * 4 + i - 1
            sr[i, p] = uf[pl.ds(p * 8 + jnp.clip(theirs, 0, 7), EL, stride=16), :].astype(BF16)
        return carry

    lax.fori_loop(0, 6, half_step, 0)
    W[1, 5 * zh] = jnp.zeros((2, EL, 128), BF16)

    @pl.when(s == 0)
    def _():
        H[:, 0] = jnp.zeros((2, 4, EL, 128), BF16)

    @pl.when(s == 15)
    def _():
        H[:, 1] = jnp.zeros((2, 4, EL, 128), BF16)

    start_halo(0)
    def electrodes(i, origin):
        _, lo, n = PIECES[i]
        return pl.ds(pl.multiple_of(origin * EL + lo, 64), n)

    def group(i):
        return e if PIECES[i][0] == 0 else partner

    def field_copy(i, d, part):
        g, lo, n = PIECES[i]
        tx = lax.rem(x + d, 4)
        cols = pl.ds(0, 512) if part == 0 else pl.ds(512, 256)
        return remote(sb.at[g, tx, lo:lo + n, cols], S.at[electrodes(i, group(i)), cols],
                      fs.at[i, part, d - 1], fr.at[i, part, d - 1], x_peer(d))

    def zy_slopes(i):
        g, lo, n = PIECES[i]
        rows = slice(lo, lo + n)
        lane = lax.broadcasted_iota(jnp.int32, (n, 128), 1)

        def step(j, carry):
            t = lax.rem(x + j, 4)
            for p in range(2):
                u = W[g, t + 1, p, rows].astype(F32)
                before, after = W[g, t, p, rows].astype(F32), W[g, t + 2, p, rows].astype(F32)
                left = jnp.where(lane > 0, pltpu.roll(u, 1, axis=1), 0.0)
                right = jnp.where(lane < 127, pltpu.roll(u, 127, axis=1), 0.0)
                sb[g, t, rows, p * 128:p * 128 + 128] = (0.5 * (right - left)).astype(BF16)
                sb[g, t, rows, 256 + p * 128:256 + p * 128 + 128] = (0.5 * (after - before)).astype(BF16)

            @pl.when(j < 4)
            def _():
                field_copy(i, j, 0).start()

            return carry

        lax.fori_loop(1, 5, step, 0)

    def x_slopes(i):
        g, lo, n = PIECES[i]
        rows = slice(lo, lo + n)

        def step(j, carry):
            t = lax.rem(x + j, 4)
            u0, u1 = W[g, t + 1, 0, rows].astype(F32), W[g, t + 1, 1, rows].astype(F32)
            low, high = H[g, 0, t, rows].astype(F32), H[g, 1, t, rows].astype(F32)
            sb[g, t, rows, 512:640] = (0.5 * (u1 - low)).astype(BF16)
            sb[g, t, rows, 640:768] = (0.5 * (high - u0)).astype(BF16)

            @pl.when(j < 4)
            def _():
                field_copy(i, j, 1).start()

            return carry

        lax.fori_loop(1, 5, step, 0)
        S[electrodes(i, group(i)), :] = sb[g, x, rows]

    def forward(i, d):
        origin = (zh if PIECES[i][0] == 0 else 1 - zh) * 8 + lax.rem(x + 4 - d, 4) * 2 + c
        rows = electrodes(i, origin)
        return remote(S.at[rows], S.at[rows], ws.at[i, d], wr.at[i, d], other_core)

    def slab(a, b):
        return pl.ds(pl.multiple_of((a * 4 + b) * ROWS, 16), ROWS)

    def slab_copy(d):
        a = Tb.at[:, slab(y, x)]
        return remote(a, a, p2_s.at[d - 1], p2_r.at[d - 1], x_peer(d))

    def wide_copy(d, dy):
        a = Tb.at[:, slab(y, lax.rem(x + 4 - d, 4))]
        return remote(a, a, p3_s.at[d, dy - 1], p3_r.at[d, dy - 1], y_peer(dy))

    def relay_copy(d, half):
        a = Tb.at[half * 4:half * 4 + 4, slab(lax.rem(y + (3, 1)[half], 4), lax.rem(x + 4 - d, 4))]
        return remote(a, a, p4_s.at[d, half], p4_r.at[d, half], y_peer((1, 3)[half]))

    def relay(d):
        for half, dy in ((0, 1), (1, 3)):
            wide_copy(d, dy).wait_recv()
            relay_copy(d, half).start()

    def pass_on(i, d):
        field_copy(i, d, 0).wait_recv()
        field_copy(i, d, 1).wait_recv()
        forward(i, d).start()

    def start_all(copies):
        for copy in copies:
            copy.start()

    def arrived(copies):
        for copy in copies:
            copy.wait_recv()

    arrived(z_copy(d) for d in range(1, 8))
    raw_copy(1).start()
    start_all(slab_copy(d) for d in (1, 3, 2))
    start_all(wide_copy(0, dy) for dy in (1, 3))
    slab_copy(1).wait_recv()
    start_all(wide_copy(1, dy) for dy in (1, 3))
    zy_slopes(0)
    halo_arrived(0)
    x_slopes(0)
    forward(0, 0).start()
    slab_copy(3).wait_recv()
    start_all(wide_copy(3, dy) for dy in (1, 3))
    raw_copy(1).wait_recv()
    start_halo(1)
    zy_slopes(1)
    slab_copy(2).wait_recv()
    start_all(wide_copy(2, dy) for dy in (1, 3))
    halo_arrived(1)
    x_slopes(1)
    forward(1, 0).start()
    relay(0)
    relay(1)
    relay(3)
    for d in (1, 3, 2):
        pass_on(0, d)
    relay(2)
    for d in (1, 3, 2):
        pass_on(1, d)
    for i in range(2):
        arrived(forward(i, d) for d in range(4))

    def product(jj, k, acc):
        rows = pl.ds(pl.multiple_of(k * 4 * ROWS, 16), 4 * ROWS)
        lhs = jnp.concatenate([Tb[2 * jj, rows], Tb[2 * jj + 1, rows]], axis=1)
        first = (c * 4 + jj) * 256
        for n in range(3):
            cols = slice(n * 256, n * 256 + 256)
            image = jnp.dot(lhs, S[pl.ds(pl.multiple_of(first, 256), 256), cols], preferred_element_type=F32)
            for b in range(5):
                own_rows = pl.ds(pl.multiple_of((first + k * 4 * ROWS + b * 64) & (E - 1), 64), 64)
                prod = image[b * 64:b * 64 + 64] * S[own_rows, cols].astype(F32)
                acc = acc + jnp.sum(prod.reshape(8, 8, 256), axis=0)
        return acc

    total = jnp.zeros((8, 256), F32)
    for d in (0, 1, 3, 2):
        if d == 2:
            arrived(relay_copy(o, half) for o in range(4) for half in range(2))
        total = lax.fori_loop(0, 4, lambda jj, acc: product(jj, lax.rem(y + 4 - d, 4), acc), total)
    total = jnp.sum(total, axis=0, keepdims=True)
    gs[...] = jnp.zeros((8, 128), F32)
    gs[0:1, :] = total[:, 0:128]
    gs[1:2, :] = total[:, 128:256]

    cores = remote(gs, gx, c_s, c_r, other_core)
    cores.start()
    cores.wait_recv()
    gt[...] = gs[...] + gx[...]

    def share(k):
        return remote(gt, gr.at[mi], g_s.at[k - 1], g_r.at[k - 1], chip_peer(k))

    for k in (4, 3, 5, 2, 6, 1, 7):
        share(k).start()
    gr[mi] = gt[...]
    for k in range(1, 8):
        share(k).wait_recv()
    for m in range(8):
        for p in range(2):
            out[p, m:m + 1, :] = gr[m, p:p + 1, :] * weight[p, m:m + 1, :]

    sent = [raw_copy(1)]
    for i in range(2):
        halo_sent(i)
        sent += [field_copy(i, d, part) for d in range(1, 4) for part in range(2)]
        sent += [forward(i, d) for d in range(4)]
    sent += [z_copy(d) for d in range(1, 8)]
    for d in range(1, 4):
        sent += [slab_copy(d)]
    for o in range(4):
        sent += [wide_copy(o, dy) for dy in (1, 3)] + [relay_copy(o, half) for half in range(2)]
    sent += [cores] + [share(k) for k in range(1, 8)]
    for copy in sent:
        copy.wait_send()


def local(potentials, quadrupoles, residuals, cell_weight):
    dma = pltpu.SemaphoreType.DMA
    return pl.pallas_call(
        kernel,
        name="misfit_gradient",
        out_shape=jax.ShapeDtypeStruct(cell_weight.shape, F32),
        in_specs=[pl.BlockSpec(memory_space=pltpu.VMEM)] * 4,
        out_specs=pl.BlockSpec(memory_space=pltpu.VMEM),
        scratch_shapes=[
            pltpu.VMEM((EL * 16, 128), F32),
            pltpu.VMEM((2, 6, 2, EL, 128), BF16),
            pltpu.VMEM((6, 2, EL, 128), BF16),
            pltpu.VMEM((2, 2, 4, EL, 128), BF16),
            pltpu.VMEM((2, 4, EL, NC), BF16),
            pltpu.VMEM((E, NC), BF16),
            pltpu.VMEM((8, WIN, 128), BF16),
            pltpu.VMEM((8, 128), F32),
            pltpu.VMEM((8, 128), F32),
            pltpu.VMEM((8, 128), F32),
            pltpu.VMEM((8, 8, 128), F32),
            dma((2,)), dma((2,)),
            dma((3, 2)), dma((3, 2)),
            dma((3, 2, 3)), dma((3, 2, 3)),
            dma((3, 4)), dma((3, 4)),
            dma((7,)), dma((7,)),
            dma((3,)), dma((3,)),
            dma((4, 3)), dma((4, 3)),
            dma((4, 2)), dma((4, 2)),
            dma(()), dma(()),
            dma((7,)), dma((7,)),
        ],
        compiler_params=pltpu.CompilerParams(
            collective_id=0, has_side_effects=True, vmem_limit_bytes=56 << 20),
    )(potentials, quadrupoles, residuals.reshape(1, QUADS), cell_weight)


def solution(mesh):
    placed = (P("elec", "space", None, None), P(), P(), P("space", None, None))
    return jax.shard_map(
        local, mesh=mesh, in_specs=placed, out_specs=P("space", None, None), check_vma=False
    )
```

```python
import jax
import jax.numpy as jnp
from jax import lax
from jax.experimental import pallas as pl
from jax.experimental.pallas import tpu as pltpu
from jax.sharding import PartitionSpec as P

MESH = pl.DeviceIdType.MESH
F32 = jnp.float32
BF16 = jnp.bfloat16
E = 2048
EL = 128
QUADS = 32768
QK = 4096
ROWS = 80
WIN = 1280
PIECES = ((0, 0, 128), (1, 0, 128))
NC = 768


def kernel(pot, quad, res, weight, out,
           uf, W, sr, H, sb, S, Tb, gs, gx, gt, gr,
           r_s, r_r, halo_s, halo_r, fs, fr, ws, wr, z_s, z_r, p2_s, p2_r, p3_s, p3_r, p4_s, p4_r, c_s, c_r, g_s, g_r):
    e = lax.axis_index("elec")
    s = lax.axis_index("space")
    zh, x, c = e // 8, (e // 2) % 4, e % 2
    zl, y = s // 4, s % 4
    z = zh * 4 + zl
    mi = zh * 4 + x

    def chip_peer(k):
        return (lax.rem(mi + k, 8) * 2 + c, s)

    def space_peer(d):
        return (e, lax.rem(s + d + 16, 16))

    def z_peer(d):
        t = lax.rem(z + d, 8)
        return ((t // 4) * 8 + x * 2 + c, lax.rem(t, 4) * 4 + y)

    def x_peer(d):
        return (zh * 8 + lax.rem(x + d, 4) * 2 + c, s)

    def y_peer(d):
        return (e, zl * 4 + lax.rem(y + d, 4))

    other_core = (zh * 8 + x * 2 + (1 - c), s)
    partner = lax.rem(e + 8, 16)

    def remote(src, dst, ss, rs, device):
        return pltpu.make_async_remote_copy(
            src_ref=src, dst_ref=dst, send_sem=ss, recv_sem=rs, device_id=device, device_id_type=MESH)

    barrier = pltpu.get_barrier_semaphore()
    peers = ([chip_peer(k) for k in range(1, 8)] + [other_core, space_peer(1), space_peer(-1)]
             + [z_peer(d) for d in (1, 2, 3, 5, 6, 7)] + [y_peer(d) for d in (1, 2, 3)])
    for peer in peers:
        pl.semaphore_signal(barrier, inc=1, device_id=peer, device_id_type=MESH)

    rb = y * 4 + x
    col0 = c * 1024 + z * 128
    row0 = (c * 4 + z // 2) * 256 + rb * ROWS
    row_ids = ((lax.broadcasted_iota(jnp.int32, (ROWS, QK), 0) + row0) & (E - 1)).astype(jnp.int16)
    col_ids = (lax.broadcasted_iota(jnp.int32, (EL, QK), 0) + col0).astype(jnp.int16)
    one = jnp.ones((16, QK), BF16)
    zero = jnp.zeros((16, QK), BF16)

    def hot(u, v, ids, plus, minus):
        return jnp.concatenate(
            [jnp.where(u == ids[k:k + 16], plus, jnp.where(v == ids[k:k + 16], minus, zero))
             for k in range(0, ids.shape[0], 16)], axis=0)

    def nt(a, b):
        return lax.dot_general(a, b, (((1,), (1,)), ((), ())), preferred_element_type=F32)

    def quad_step(i, acc):
        q = pl.ds(pl.multiple_of(i * QK, QK), QK)
        a, b, m, n = (quad[k:k + 1, q] for k in range(4))
        r = jnp.where((a == b) | (m == n), 0.0, res[0:1, q])
        a, b, m, n = (jnp.broadcast_to(v, (16, QK)).astype(jnp.int16) for v in (a, b, m, n))
        r = jnp.broadcast_to(r, (16, QK)).astype(BF16)
        acc = acc + nt(hot(a, b, row_ids, one, -one), hot(m, n, col_ids, r, -r))
        return acc + nt(hot(m, n, row_ids, one, -one), hot(a, b, col_ids, r, -r))

    block = lax.fori_loop(0, QUADS // QK, quad_step, jnp.zeros((ROWS, EL), F32))
    offset = lax.broadcasted_iota(jnp.int32, (ROWS, EL), 0) + rb * ROWS
    block = jnp.where((offset < 256) | (offset >= 1024), 0.5 * block, block)
    own = pl.ds(pl.multiple_of(rb * ROWS, 16), ROWS)
    Tb[z, own, :] = block.astype(BF16)

    pl.semaphore_wait(barrier, len(peers))

    raw = pl.ds(zh, 5)

    def raw_copy(i):
        _, lo, n = PIECES[i]
        return remote(sr.at[raw, :, lo:lo + n], W.at[1, raw, :, lo:lo + n], r_s.at[i - 1], r_r.at[i - 1], (partner, s))

    def halo_copies(i):
        g, lo, n = PIECES[i]
        return (remote(W.at[g, 1:5, 1, lo:lo + n], H.at[g, 0, :, lo:lo + n],
                       halo_s.at[i, 0], halo_r.at[i, 0], space_peer(1)),
                remote(W.at[g, 1:5, 0, lo:lo + n], H.at[g, 1, :, lo:lo + n],
                       halo_s.at[i, 1], halo_r.at[i, 1], space_peer(-1)))

    def start_halo(i):
        up, down = halo_copies(i)

        @pl.when(s < 15)
        def _():
            up.start()

        @pl.when(s > 0)
        def _():
            down.start()

    def halo_arrived(i):
        up, down = halo_copies(i)

        @pl.when(s > 0)
        def _():
            up.wait_recv()

        @pl.when(s < 15)
        def _():
            down.wait_recv()

    def halo_sent(i):
        up, down = halo_copies(i)

        @pl.when(s < 15)
        def _():
            up.wait_send()

        @pl.when(s > 0)
        def _():
            down.wait_send()

    def z_copy(d):
        return remote(Tb.at[z, own], Tb.at[z, own], z_s.at[d - 1], z_r.at[d - 1], z_peer(d))

    for d in (4, 3, 5, 2, 6, 1, 7):
        z_copy(d).start()
    uf[...] = pot[...].astype(F32).reshape(EL * 16, 128)

    def half_step(i, carry):
        for p in range(2):
            mine = zh * 4 + i - 1
            u = uf[pl.ds(p * 8 + jnp.clip(mine, 0, 7), EL, stride=16), :]
            W[0, i, p] = jnp.where((mine >= 0) & (mine < 8), u, 0.0).astype(BF16)
            theirs = (1 - zh) * 4 + i - 1
            sr[i, p] = uf[pl.ds(p * 8 + jnp.clip(theirs, 0, 7), EL, stride=16), :].astype(BF16)
        return carry

    lax.fori_loop(0, 6, half_step, 0)
    W[1, 5 * zh] = jnp.zeros((2, EL, 128), BF16)

    @pl.when(s == 0)
    def _():
        H[:, 0] = jnp.zeros((2, 4, EL, 128), BF16)

    @pl.when(s == 15)
    def _():
        H[:, 1] = jnp.zeros((2, 4, EL, 128), BF16)

    start_halo(0)
    def electrodes(i, origin):
        _, lo, n = PIECES[i]
        return pl.ds(pl.multiple_of(origin * EL + lo, 64), n)

    def group(i):
        return e if PIECES[i][0] == 0 else partner

    def field_copy(i, d, part):
        g, lo, n = PIECES[i]
        tx = lax.rem(x + d, 4)
        cols = pl.ds(0, 512) if part == 0 else pl.ds(512, 256)
        return remote(sb.at[g, tx, lo:lo + n, cols], S.at[electrodes(i, group(i)), cols],
                      fs.at[i, part, d - 1], fr.at[i, part, d - 1], x_peer(d))

    def zy_slopes(i):
        g, lo, n = PIECES[i]
        rows = slice(lo, lo + n)
        lane = lax.broadcasted_iota(jnp.int32, (n, 128), 1)

        def step(j, carry):
            t = lax.rem(x + j, 4)
            for p in range(2):
                u = W[g, t + 1, p, rows].astype(F32)
                before, after = W[g, t, p, rows].astype(F32), W[g, t + 2, p, rows].astype(F32)
                left = jnp.where(lane > 0, pltpu.roll(u, 1, axis=1), 0.0)
                right = jnp.where(lane < 127, pltpu.roll(u, 127, axis=1), 0.0)
                sb[g, t, rows, p * 128:p * 128 + 128] = (0.5 * (right - left)).astype(BF16)
                sb[g, t, rows, 256 + p * 128:256 + p * 128 + 128] = (0.5 * (after - before)).astype(BF16)

            @pl.when(j < 4)
            def _():
                field_copy(i, j, 0).start()

            return carry

        lax.fori_loop(1, 5, step, 0)

    def x_slopes(i):
        g, lo, n = PIECES[i]
        rows = slice(lo, lo + n)

        def step(j, carry):
            t = lax.rem(x + j, 4)
            u0, u1 = W[g, t + 1, 0, rows].astype(F32), W[g, t + 1, 1, rows].astype(F32)
            low, high = H[g, 0, t, rows].astype(F32), H[g, 1, t, rows].astype(F32)
            sb[g, t, rows, 512:640] = (0.5 * (u1 - low)).astype(BF16)
            sb[g, t, rows, 640:768] = (0.5 * (high - u0)).astype(BF16)

            @pl.when(j < 4)
            def _():
                field_copy(i, j, 1).start()

            return carry

        lax.fori_loop(1, 5, step, 0)
        S[electrodes(i, group(i)), :] = sb[g, x, rows]

    def forward(i, d):
        origin = (zh if PIECES[i][0] == 0 else 1 - zh) * 8 + lax.rem(x + 4 - d, 4) * 2 + c
        rows = electrodes(i, origin)
        return remote(S.at[rows], S.at[rows], ws.at[i, d], wr.at[i, d], other_core)

    def slab(a, b):
        return pl.ds(pl.multiple_of((a * 4 + b) * ROWS, 16), ROWS)

    def slab_copy(d):
        a = Tb.at[:, slab(y, x)]
        return remote(a, a, p2_s.at[d - 1], p2_r.at[d - 1], x_peer(d))

    def wide_copy(d, dy):
        a = Tb.at[:, slab(y, lax.rem(x + 4 - d, 4))]
        return remote(a, a, p3_s.at[d, dy - 1], p3_r.at[d, dy - 1], y_peer(dy))

    def relay_copy(d, half):
        a = Tb.at[half * 4:half * 4 + 4, slab(lax.rem(y + (3, 1)[half], 4), lax.rem(x + 4 - d, 4))]
        return remote(a, a, p4_s.at[d, half], p4_r.at[d, half], y_peer((1, 3)[half]))

    def relay(d):
        for half, dy in ((0, 1), (1, 3)):
            wide_copy(d, dy).wait_recv()
            relay_copy(d, half).start()

    def pass_on(i, d):
        field_copy(i, d, 0).wait_recv()
        field_copy(i, d, 1).wait_recv()
        forward(i, d).start()

    def start_all(copies):
        for copy in copies:
            copy.start()

    def arrived(copies):
        for copy in copies:
            copy.wait_recv()

    arrived(z_copy(d) for d in range(1, 8))
    raw_copy(1).start()
    start_all(slab_copy(d) for d in (1, 3, 2))
    start_all(wide_copy(0, dy) for dy in (1, 3))
    slab_copy(1).wait_recv()
    start_all(wide_copy(1, dy) for dy in (1, 3))
    zy_slopes(0)
    halo_arrived(0)
    x_slopes(0)
    forward(0, 0).start()
    slab_copy(3).wait_recv()
    start_all(wide_copy(3, dy) for dy in (1, 3))
    slab_copy(2).wait_recv()
    start_all(wide_copy(2, dy) for dy in (1, 3))
    raw_copy(1).wait_recv()
    start_halo(1)
    zy_slopes(1)
    halo_arrived(1)
    x_slopes(1)
    forward(1, 0).start()
    relay(0)
    relay(1)
    relay(3)
    for d in (1, 3, 2):
        pass_on(0, d)
    relay(2)
    for d in (1, 3, 2):
        pass_on(1, d)
    for i in range(2):
        arrived(forward(i, d) for d in range(4))

    def product(jj, k, acc):
        rows = pl.ds(pl.multiple_of(k * 4 * ROWS, 16), 4 * ROWS)
        lhs = jnp.concatenate([Tb[2 * jj, rows], Tb[2 * jj + 1, rows]], axis=1)
        first = (c * 4 + jj) * 256
        for n in range(3):
            cols = slice(n * 256, n * 256 + 256)
            image = jnp.dot(lhs, S[pl.ds(pl.multiple_of(first, 256), 256), cols], preferred_element_type=F32)
            for b in range(5):
                own_rows = pl.ds(pl.multiple_of((first + k * 4 * ROWS + b * 64) & (E - 1), 64), 64)
                prod = image[b * 64:b * 64 + 64] * S[own_rows, cols].astype(F32)
                acc = acc + jnp.sum(prod.reshape(8, 8, 256), axis=0)
        return acc

    total = jnp.zeros((8, 256), F32)
    for d in (0, 1, 3, 2):
        if d == 2:
            arrived(relay_copy(o, half) for o in range(4) for half in range(2))
        total = lax.fori_loop(0, 4, lambda jj, acc: product(jj, lax.rem(y + 4 - d, 4), acc), total)
    total = jnp.sum(total, axis=0, keepdims=True)
    gs[...] = jnp.zeros((8, 128), F32)
    gs[0:1, :] = total[:, 0:128]
    gs[1:2, :] = total[:, 128:256]

    cores = remote(gs, gx, c_s, c_r, other_core)
    cores.start()
    cores.wait_recv()
    gt[...] = gs[...] + gx[...]

    def share(k):
        return remote(gt, gr.at[mi], g_s.at[k - 1], g_r.at[k - 1], chip_peer(k))

    for k in (4, 3, 5, 2, 6, 1, 7):
        share(k).start()
    gr[mi] = gt[...]
    for k in range(1, 8):
        share(k).wait_recv()
    for m in range(8):
        for p in range(2):
            out[p, m:m + 1, :] = gr[m, p:p + 1, :] * weight[p, m:m + 1, :]

    sent = [raw_copy(1)]
    for i in range(2):
        halo_sent(i)
        sent += [field_copy(i, d, part) for d in range(1, 4) for part in range(2)]
        sent += [forward(i, d) for d in range(4)]
    sent += [z_copy(d) for d in range(1, 8)]
    for d in range(1, 4):
        sent += [slab_copy(d)]
    for o in range(4):
        sent += [wide_copy(o, dy) for dy in (1, 3)] + [relay_copy(o, half) for half in range(2)]
    sent += [cores] + [share(k) for k in range(1, 8)]
    for copy in sent:
        copy.wait_send()


def local(potentials, quadrupoles, residuals, cell_weight):
    dma = pltpu.SemaphoreType.DMA
    return pl.pallas_call(
        kernel,
        name="misfit_gradient",
        out_shape=jax.ShapeDtypeStruct(cell_weight.shape, F32),
        in_specs=[pl.BlockSpec(memory_space=pltpu.VMEM)] * 4,
        out_specs=pl.BlockSpec(memory_space=pltpu.VMEM),
        scratch_shapes=[
            pltpu.VMEM((EL * 16, 128), F32),
            pltpu.VMEM((2, 6, 2, EL, 128), BF16),
            pltpu.VMEM((6, 2, EL, 128), BF16),
            pltpu.VMEM((2, 2, 4, EL, 128), BF16),
            pltpu.VMEM((2, 4, EL, NC), BF16),
            pltpu.VMEM((E, NC), BF16),
            pltpu.VMEM((8, WIN, 128), BF16),
            pltpu.VMEM((8, 128), F32),
            pltpu.VMEM((8, 128), F32),
            pltpu.VMEM((8, 128), F32),
            pltpu.VMEM((8, 8, 128), F32),
            dma((2,)), dma((2,)),
            dma((3, 2)), dma((3, 2)),
            dma((3, 2, 3)), dma((3, 2, 3)),
            dma((3, 4)), dma((3, 4)),
            dma((7,)), dma((7,)),
            dma((3,)), dma((3,)),
            dma((4, 3)), dma((4, 3)),
            dma((4, 2)), dma((4, 2)),
            dma(()), dma(()),
            dma((7,)), dma((7,)),
        ],
        compiler_params=pltpu.CompilerParams(
            collective_id=0, has_side_effects=True, vmem_limit_bytes=56 << 20),
    )(potentials, quadrupoles, residuals.reshape(1, QUADS), cell_weight)


def solution(mesh):
    placed = (P("elec", "space", None, None), P(), P(), P("space", None, None))
    return jax.shard_map(
        local, mesh=mesh, in_specs=placed, out_specs=P("space", None, None), check_vma=False
    )
```
